128 devices in a mesh: grp: 2 (over x_lo), tile: 64 (over z, y, x_hi, core).
Axes of the slice: x: 4 (x_hi: 2, x_lo: 2; x = x_hi * 2 + x_lo), y: 4, z: 4, core: 2. Of those that a mesh axis runs over, the one named last changes fastest.
Arguments:
- ocean_state: float32 [3, 24, 1024, 4096], P(None, None, 'tile', 'grp'), may hold values from -6 to 6
- biharmonic: float32 [1024, 4096], P('tile', 'grp'), may hold values from 0.004 to 0.014
- prev_stress: float32 [2, 1024, 4096], P(None, 'tile', 'grp'), may hold values from -4 to 4
- ice_state: float32 [5, 1024, 4096], P(None, 'tile', 'grp'), may hold values from -2 to 2
- strength: float32 [1024, 4096], P('tile', 'grp'), may hold values from 0.5 to 2
- ice_mass: float32 [1024, 4096], P('tile', 'grp'), may hold values from 0.5 to 2
- ice_fraction: float32 [1024, 4096], P('tile', 'grp'), may hold values from 0.15 to 1
- wind_stress: float32 [2, 1024, 4096], P(None, 'tile', 'grp'), may hold values from -2 to 2
- ice_count: int32 [128], P(('grp', 'tile')), may hold values from 0 to 16, as said below
- ice_list: int32 [128, 16], P(('grp', 'tile')), may hold values from 0 to 15, as said below
Outputs:
- ocean_out: float32 [3, 24, 1024, 4096], P(None, None, 'tile', 'grp')
- ice_out: float32 [5, 1024, 4096], P(None, 'tile', 'grp')
- stress_out: float32 [2, 1024, 4096], P(None, 'tile', 'grp')
The draws below stay inside these ranges and needn't reach their ends.
Inputs may be any that keep to these rules, and one draw needn't show every extreme that they name: `ice_count`: the tiles g * 64 + t and g * 64 + (t + 64 / 2) % 64 together have at most 16 ice-covered blocks, and some such pair has exactly 16; tiles near the first and last rows have the most. `ice_list`: each row is an ordering of the tile's 16 block numbers.
All inputs are finite; a program needn't handle non-finite values.
Results may differ from the reference program's by a relative error of at most 0.00002.
Values sent between devices are 32-bit elements; how exact they have to be, the bound alone decides.
A program may use at most 192 MiB of HBM per device.

```python
import math
import jax
import jax.numpy as jnp
from jax import lax

LEV = 24
CY = 16
CX = 2048
BY = 16
BX = 128
SUBCYCLES = 64
NY = 1024
NX = 4096
OWNERS = 128
NB_DEV = 16
N_GRP = 2
N_TILE = 64


def ice_layout(key):
    quarter = N_TILE // 4
    halfway = N_TILE // 2
    base = jnp.arange(halfway, dtype=jnp.int32)
    polar = jnp.minimum(base, halfway - 1 - base)
    spread = 1 + polar * (NB_DEV // 2) // quarter
    first_key, second_key = jax.random.split(jax.random.fold_in(key, 11))
    reduction = jax.random.randint(first_key, (N_GRP, halfway), 0, spread[None, :])
    heavy = NB_DEV - reduction
    light = jax.random.randint(second_key, (N_GRP, halfway), 0, NB_DEV - heavy + 1)
    first_heavy = (base < quarter)[None, :]
    first = jnp.where(first_heavy, heavy, light)
    second = jnp.where(first_heavy, light, heavy)
    return jnp.concatenate([first, second], axis=1).reshape(N_GRP * N_TILE).astype(jnp.int32)


def draw_ice_count(key, part):
    return ice_layout(key)


def draw_ice_list(key, part):
    scores = jax.random.randint(jax.random.fold_in(key, 23), (OWNERS, NB_DEV), 0, 1 << 20)
    scores = scores * NB_DEV + jnp.arange(NB_DEV, dtype=jnp.int32)[None, :]
    return jnp.argsort(scores, axis=1).astype(jnp.int32)


def shard_levels(stream_key, extent, shards, least, largest):
    level = 1.0
    for dim, parts in shards:
        draws = jax.random.uniform(jax.random.fold_in(jax.random.fold_in(stream_key, 6), dim), (parts,), jnp.float32, least / len(shards), largest / len(shards))
        level = level * jnp.repeat(jnp.exp(draws), extent[dim] // parts).reshape((-1,) + (1,) * (len(extent) - 1 - dim))
    return level


def scatter_about(rng, dims, scale, bound, cuts=(), kind=jnp.bfloat16):
    factor_of = shard_levels(rng, dims, cuts, -0.22, 0.18) if cuts else 1.0
    drawn = jax.random.normal(rng, dims, jnp.float32) * scale * factor_of
    return jnp.minimum(jnp.maximum(drawn, -bound), bound).astype(kind)


def setup_inputs(seed: int = 0) -> dict:
    streams_of = jax.random.split(jax.random.key(seed), 11)
    return {
        "ocean_state": scatter_about(streams_of[0], (3, LEV, NY, NX), 1.0, 6.0, ((2, 64), (3, 2)), jnp.float32),
        "biharmonic": jnp.clip(jnp.exp(math.log(0.014) - 1.25276295 * jax.random.uniform(streams_of[1], (NY, NX), jnp.float32) ** shard_levels(streams_of[1], (NY, NX), ((0, 64), (1, 2)), -0.2, 0.2)), 0.004, 0.014),
        "prev_stress": scatter_about(streams_of[2], (2, NY, NX), 0.5, 4.0, ((1, 64), (2, 2)), jnp.float32),
        "ice_state": scatter_about(streams_of[3], (5, NY, NX), 0.3, 2.0, ((1, 64), (2, 2)), jnp.float32),
        "strength": jnp.clip(jnp.exp(math.log(2.0) - 1.3862944 * jax.random.uniform(streams_of[4], (NY, NX), jnp.float32) ** shard_levels(streams_of[4], (NY, NX), ((0, 64), (1, 2)), -0.2, 0.2)), 0.5, 2.0),
        "ice_mass": jnp.clip(jnp.exp(math.log(2.0) - 1.3862944 * jax.random.uniform(streams_of[5], (NY, NX), jnp.float32) ** shard_levels(streams_of[5], (NY, NX), ((0, 64), (1, 2)), -0.2, 0.2)), 0.5, 2.0),
        "ice_fraction": jnp.clip(0.15 + 0.85 * jax.random.uniform(streams_of[6], (NY, NX), jnp.float32) ** shard_levels(streams_of[6], (NY, NX), ((0, 64), (1, 2)), -0.2, 0.2), 0.15, 1.0),
        "wind_stress": scatter_about(streams_of[7], (2, NY, NX), 0.3, 2.0, ((1, 64), (2, 2)), jnp.float32),
        "ice_count": draw_ice_count(jax.random.fold_in(streams_of[10], 71), 0),
        "ice_list": draw_ice_list(jax.random.fold_in(streams_of[10], 71), 0),
    }


kv_mix = 0.2
relax_rate = 0.5
sub_step = 0.3
drag_coef = 1.0
turning = 0.3
delta_min = 0.5
coriolis_scale = 0.2

def ahead_diff(field, axis):
    length = field.shape[axis]
    inner = lax.slice_in_dim(field, 1, length, axis=axis) - lax.slice_in_dim(field, 0, length - 1, axis=axis)
    return jnp.concatenate([inner, jnp.zeros_like(lax.slice_in_dim(field, 0, 1, axis=axis))], axis=axis)

def behind_diff(field, axis):
    length = field.shape[axis]
    inner = lax.slice_in_dim(field, 1, length, axis=axis) - lax.slice_in_dim(field, 0, length - 1, axis=axis)
    return jnp.concatenate([lax.slice_in_dim(field, 0, 1, axis=axis), inner], axis=axis)

def ice_dynamics(fields, y_axis, x_axis):
    vel_x, vel_y, stress_xx, stress_yy, stress_xy, ice_strength, mass, fraction, wind_x, wind_y, ocean_x, ocean_y = fields
    pressure = relax_rate * ice_strength
    inertia = mass + sub_step * drag_coef

    def subcycle(step_index, carry):
        vel_x, vel_y, stress_xx, stress_yy, stress_xy = carry
        du_dx = ahead_diff(vel_x, x_axis)
        du_dy = ahead_diff(vel_x, y_axis)
        dv_dx = ahead_diff(vel_y, x_axis)
        dv_dy = ahead_diff(vel_y, y_axis)
        divergence = du_dx + dv_dy
        tension = du_dx - dv_dy
        shearing = du_dy + dv_dx
        deform = jnp.sqrt(divergence * divergence + 0.25 * (tension * tension + shearing * shearing) + delta_min * delta_min)
        sigma_one = (stress_xx + stress_yy + pressure * (divergence / deform - 1.0)) / (1.0 + relax_rate)
        sigma_two = (stress_xx - stress_yy + 0.25 * pressure * tension / deform) / (1.0 + relax_rate)
        stress_xy = (stress_xy + 0.125 * pressure * shearing / deform) / (1.0 + relax_rate)
        stress_xx = 0.5 * (sigma_one + sigma_two)
        stress_yy = 0.5 * (sigma_one - sigma_two)
        force_x = behind_diff(stress_xx, x_axis) + behind_diff(stress_xy, y_axis)
        force_y = behind_diff(stress_xy, x_axis) + behind_diff(stress_yy, y_axis)
        new_x = (mass * vel_x + sub_step * (force_x + wind_x + drag_coef * ocean_x + turning * mass * vel_y)) / inertia
        new_y = (mass * vel_y + sub_step * (force_y + wind_y + drag_coef * ocean_y - turning * mass * vel_x)) / inertia
        return (new_x, new_y, stress_xx, stress_yy, stress_xy)
    vel_x, vel_y, stress_xx, stress_yy, stress_xy = lax.fori_loop(0, SUBCYCLES, subcycle, (vel_x, vel_y, stress_xx, stress_yy, stress_xy))
    drag_x = fraction * drag_coef * (vel_x - ocean_x) + (1.0 - fraction) * wind_x
    drag_y = fraction * drag_coef * (vel_y - ocean_y) + (1.0 - fraction) * wind_y
    return (vel_x, vel_y, stress_xx, stress_yy, stress_xy, drag_x, drag_y)

def laplace(padded):
    return padded[..., 1:-1, 2:] + padded[..., 1:-1, :-2] + padded[..., 2:, 1:-1] + padded[..., :-2, 1:-1] - 4.0 * padded[..., 1:-1, 1:-1]

def vertical(field):
    upper = jnp.concatenate([field[:1], field[:-1]], axis=0)
    lower = jnp.concatenate([field[1:], field[-1:]], axis=0)
    return upper + lower - 2.0 * field

def ocean_field(padded, field, biharmonic):
    return field - biharmonic * laplace(laplace(padded)) + kv_mix * vertical(field)

def pad_ocean(field):
    padded = jnp.pad(field, ((0, 0), (2, 2), (0, 0)))
    return jnp.concatenate([padded[..., -2:], padded, padded[..., :2]], axis=-1)

def reference(ocean_state, biharmonic, prev_stress, ice_state, strength, ice_mass, ice_fraction, wind_stress, ice_count, ice_list):
    rows = jnp.arange(NY).astype(jnp.float32) + 0.5
    coriolis = (coriolis_scale * (2.0 * rows / NY - 1.0))[:, None]
    mixed = [ocean_field(pad_ocean(ocean_state[index]), ocean_state[index], biharmonic) for index in range(3)]
    east = mixed[0] + coriolis * ocean_state[1]
    north = mixed[1] - coriolis * ocean_state[0]
    east = east.at[0].add(prev_stress[0])
    north = north.at[0].add(prev_stress[1])
    ocean_out = jnp.stack([east, north, mixed[2]])
    row_blocks = NY // BY
    col_blocks = NX // BX
    grids = [ice_state[0], ice_state[1], ice_state[2], ice_state[3], ice_state[4], strength, ice_mass, ice_fraction, wind_stress[0], wind_stress[1], ocean_state[0, 0], ocean_state[1, 0]]
    fields = [grid.reshape(row_blocks, BY, col_blocks, BX) for grid in grids]
    results = ice_dynamics(fields, 1, 3)
    slots = jnp.arange(NB_DEV, dtype=jnp.int32)
    matches = ice_list[:, :, None] == slots[None, None, :]
    position = lax.optimization_barrier(jnp.sum(jnp.where(matches, slots[None, :, None], 0), axis=1))
    covered = position < ice_count[:, None]
    covered = covered.reshape(N_GRP, N_TILE, CY // BY, CX // BX).transpose(1, 2, 0, 3).reshape(row_blocks, col_blocks)
    covered = covered[:, None, :, None]
    ice_out = jnp.stack([jnp.where(covered, results[index], fields[index]).reshape(NY, NX) for index in range(5)])
    stress_out = jnp.stack([jnp.where(covered, results[5], fields[8]).reshape(NY, NX), jnp.where(covered, results[6], fields[9]).reshape(NY, NX)])
    return (ocean_out, ice_out, stress_out)
```

```python
import functools

import jax
import jax.numpy as jnp
from jax import lax
from jax.experimental import pallas as pl
from jax.experimental.pallas import tpu as pltpu
from jax.sharding import PartitionSpec as P

MESH = pl.DeviceIdType.MESH
LANES = 128
SUB = 8
SLAB = 32
SUBCYCLES = 64
THIRD = 2.0 / 3.0


def copies(refs, direction, field, group, peers):
    sbuf, rbuf, ssem, rsem = refs
    return pltpu.make_async_remote_copy(
        src_ref=sbuf.at[direction, field, group],
        dst_ref=rbuf.at[direction, field, group],
        send_sem=ssem.at[direction, field, group],
        recv_sem=rsem.at[direction, field, group],
        device_id=peers[direction],
        device_id_type=MESH,
    )


def edge_copies(refs, field, way, peers):
    esend, erecv, essem, ersem = refs
    return pltpu.make_async_remote_copy(
        src_ref=esend.at[field],
        dst_ref=erecv.at[way, field],
        send_sem=essem.at[way, field],
        recv_sem=ersem.at[way, field],
        device_id=peers[way],
        device_id_type=MESH,
    )


def kernel(
    n_tile,
    n_grp,
    ocean,
    beta,
    prev,
    ice,
    strength,
    mass,
    fraction,
    wind,
    count,
    listed,
    ocean_out,
    ice_out,
    stress_out,
    qb,
    betav,
    prevv,
    iceb,
    state,
    const,
    sbuf,
    rbuf,
    esend,
    erecv,
    qsem,
    bsem,
    isem,
    ssem,
    rsem,
    essem,
    ersem,
):
    fields, blocks, levels = ocean.shape[0], ocean.shape[3] // LANES, ocean.shape[1]
    groups = levels // SUB
    tile = lax.axis_index("tile")
    grp = lax.axis_index("grp")
    above = lax.rem(tile + 1, n_tile)
    below = lax.rem(tile + n_tile - 1, n_tile)
    other = lax.rem(grp + 1, n_grp)
    peers = [{"grp": grp, "tile": above}, {"grp": grp, "tile": below}]
    edge_peers = [
        {"grp": other, "tile": tile},
        {"grp": other, "tile": above},
        {"grp": other, "tile": below},
    ]
    row_refs = (sbuf, rbuf, ssem, rsem)
    edge_refs = (esend, erecv, essem, ersem)
    flat = qb.reshape(fields, blocks + 1, levels * SLAB, LANES)
    ice_view = iceb.reshape(12, blocks, 16, LANES)

    def columns(c):
        return pl.ds(pl.multiple_of(c * LANES, LANES), LANES)

    def load(field, c):
        return pltpu.make_async_copy(
            ocean.at[field, :, :, columns(c)], qb.at[field, c, :, 8:24, :], qsem.at[field, c]
        )

    def ice_loads(c):
        span = columns(c)
        pairs = [
            (ice.at[:, :, span], ice_view.at[0:5, c]),
            (strength.at[:, span], ice_view.at[5, c]),
            (mass.at[:, span], ice_view.at[6, c]),
            (fraction.at[:, span], ice_view.at[7, c]),
            (wind.at[:, :, span], ice_view.at[8:10, c]),
            (ocean.at[0:2, 0, :, span], ice_view.at[10:12, c]),
        ]
        return [pltpu.make_async_copy(s, d, isem.at[n, c]) for n, (s, d) in enumerate(pairs)]

    for field in range(fields):
        pl.loop(0, blocks)(lambda c, field=field: load(field, c).start())

    @pl.loop(0, blocks)
    def _(c):
        for copy in ice_loads(c):
            copy.start()

    beta_copy = pltpu.make_async_copy(beta, betav, bsem.at[0])
    prev_copy = pltpu.make_async_copy(prev, prevv, bsem.at[1])
    beta_copy.start()
    prev_copy.start()

    barrier = pltpu.get_barrier_semaphore()
    for peer in peers + edge_peers:
        pl.semaphore_signal(barrier, inc=1, device_id=peer, device_id_type=MESH)
    pl.semaphore_wait(barrier, 5)

    lane8 = lax.broadcasted_iota(jnp.int32, (SUB, LANES), 1)
    lane16 = lax.broadcasted_iota(jnp.int32, (2 * SUB, LANES), 1)
    for field in range(fields):
        pl.loop(0, blocks)(lambda c, field=field: load(field, c).wait())
        packed = jnp.zeros((2 * SUB, LANES), jnp.float32)
        for level in range(levels):
            ends = jnp.where(
                lane16 < 2, qb[field, 0, level, 8:24, :], qb[field, blocks - 1, level, 8:24, :]
            )
            ends = pltpu.roll(ends, 4 * level + 2, 1)
            packed = jnp.where(lane16 // 4 == level, ends, packed)
        esend[field] = packed
        for way in range(3):
            edge_copies(edge_refs, field, way, edge_peers).start()
        for group in range(groups):

            @pl.loop(0, blocks)
            def _(c):
                first = SLAB * SUB * group + 8
                for row in range(2):
                    sbuf[0, field, group, row, c] = flat[
                        field, c, pl.ds(first + 14 + row, SUB, stride=SLAB), :
                    ]
                    sbuf[1, field, group, row, c] = flat[
                        field, c, pl.ds(first + row, SUB, stride=SLAB), :
                    ]

            for direction in range(2):
                copies(row_refs, direction, field, group, peers).start()

    @pl.loop(0, blocks)
    def _(c):
        for copy in ice_loads(c):
            copy.wait()

    beta_copy.wait()
    prev_copy.wait()

    def ice_row(n, row):
        return jnp.stack(
            [iceb[n, pl.ds(LANES * half + row, SUB, stride=16), :] for half in range(2)]
        )

    for row in range(16):
        sxx, syy = ice_row(2, row), ice_row(3, row)
        state[0, row] = ice_row(0, row)
        state[1, row] = ice_row(1, row)
        state[2, row] = sxx + syy
        state[3, row] = 2.0 * (sxx - syy)
        state[4, row] = 4.0 * ice_row(4, row)
        m = ice_row(6, row)
        inverse = 1.0 / (m + 0.3)
        const[0, row] = (0.5 * THIRD) * ice_row(5, row)
        const[1, row] = m * inverse
        const[2, row] = 0.075 * inverse
        const[3, row] = 0.3 * inverse * (ice_row(8, row) + ice_row(10, row))
        const[4, row] = 0.3 * inverse * (ice_row(9, row) + ice_row(11, row))

    lane = lax.broadcasted_iota(jnp.int32, (2, SUB, LANES), 2)
    is_last = lane == LANES - 1
    is_first = lane == 0

    def ahead_x(q):
        return jnp.where(is_last, 0.0, pltpu.roll(q, LANES - 1, 2) - q)

    def behind_x(q):
        return q - jnp.where(is_first, 0.0, pltpu.roll(q, 1, 2))

    @pl.loop(0, SUBCYCLES)
    def _(step):
        u, v = state[0, 0], state[1, 0]
        before_xy = before_yy = None
        for row in range(16):
            du_dx, dv_dx = ahead_x(u), ahead_x(v)
            if row < 15:
                u_next, v_next = state[0, row + 1], state[1, row + 1]
                du_dy, dv_dy = u_next - u, v_next - v
                div, ten, shr = du_dx + dv_dy, du_dx - dv_dy, du_dy + dv_dx
            else:
                u_next = v_next = None
                div, ten, shr = du_dx, du_dx, dv_dx
            twice = div + div
            root = lax.rsqrt(twice * twice + ten * ten + shr * shr + 1.0)
            pressure = const[0, row]
            scaled = pressure * root
            one = THIRD * state[2, row] + (scaled * twice - pressure)
            two = THIRD * state[3, row] + scaled * ten
            xy = THIRD * state[4, row] + scaled * shr
            state[2, row] = one
            state[3, row] = two
            state[4, row] = xy
            one = one + one
            xx, yy = one + two, one - two
            force_x, force_y = behind_x(xx), behind_x(xy)
            if row:
                force_x, force_y = force_x + (xy - before_xy), force_y + (yy - before_yy)
            else:
                force_x, force_y = force_x + xy, force_y + yy
            before_xy, before_yy = xy, yy
            keep, push = const[1, row], const[2, row]
            state[0, row] = keep * (u + 0.09 * v) + (const[3, row] + push * force_x)
            state[1, row] = keep * (v - 0.09 * u) + (const[4, row] + push * force_y)
            u, v = u_next, v_next

    number = lax.broadcasted_iota(jnp.int32, (2, SUB, LANES), 0) * SUB + lax.broadcasted_iota(
        jnp.int32, (2, SUB, LANES), 1
    )
    covered = jnp.zeros((2, SUB, LANES), jnp.int32)
    for slot in range(blocks):
        block = jnp.where(slot < count[0], listed[0, slot], -1)
        covered = jnp.where(number == block, 1, covered)
    covered = covered > 0
    for row in range(16):
        u, v = state[0, row], state[1, row]
        one, two, xy = state[2, row], state[3, row], state[4, row]
        part = ice_row(7, row)
        results = {
            0: u,
            1: v,
            2: 0.5 * one + 0.25 * two,
            3: 0.5 * one - 0.25 * two,
            4: 0.25 * xy,
            8: part * (u - ice_row(10, row)) + (1.0 - part) * ice_row(8, row),
            9: part * (v - ice_row(11, row)) + (1.0 - part) * ice_row(9, row),
        }
        for n, result in results.items():
            result = jnp.where(covered, result, ice_row(n, row))
            for half in range(2):
                iceb[n, pl.ds(LANES * half + row, SUB, stride=16), :] = result[half]
    for c in range(blocks):
        span = slice(c * LANES, (c + 1) * LANES)
        for n in range(5):
            ice_out[n, :, span] = ice_view[n, c]
        for n in range(2):
            stress_out[n, :, span] = ice_view[8 + n, c]

    has_below = tile > 0
    has_above = tile < n_tile - 1
    place = (tile * 16).astype(jnp.float32) + 0.5
    place = place + lax.broadcasted_iota(jnp.int32, (16, LANES), 0).astype(jnp.float32)
    coriolis = 0.2 * (2.0 * place / (16.0 * n_tile) - 1.0)

    def masked(flag, x):
        return jnp.where(flag, x, jnp.zeros_like(x))

    @pl.loop(0, fields * groups)
    def _(chunk):
        field = lax.div(chunk, groups)
        group = lax.rem(chunk, groups)

        @pl.when(group == 0)
        def _():
            for way in range(3):
                edge_copies(edge_refs, field, way, edge_peers).wait_recv()

        for direction in range(2):
            copies(row_refs, direction, field, group, peers).wait_recv()

        @pl.loop(0, blocks)
        def _(c):
            first = pl.multiple_of(SLAB * SUB * group, SUB)
            for row in range(2):
                flat[field, c, pl.ds(first + 6 + row, SUB, stride=SLAB), :] = masked(
                    has_below, rbuf[0, field, group, row, c]
                )
                flat[field, c, pl.ds(first + 24 + row, SUB, stride=SLAB), :] = masked(
                    has_above, rbuf[1, field, group, row, c]
                )

        for inner in range(SUB):
            level = group * SUB + inner
            shift = lax.rem(2 * LANES - 2 - 4 * level, LANES)
            qb[field, blocks, level, 8:24, :] = pltpu.roll(erecv[0, field], shift, 1)
            qb[field, blocks, level, 0:8, :] = masked(
                has_below, pltpu.roll(erecv[1, field, 8:16], shift, 1)
            )
            qb[field, blocks, level, 24:32, :] = masked(
                has_above, pltpu.roll(erecv[2, field, 0:8], shift, 1)
            )

        turn = jnp.where(field == 0, 1.0, jnp.where(field == 1, -1.0, 0.0)) * coriolis
        partner = jnp.where(field == 0, 1, 0)

        @pl.loop(0, SUB)
        def _(inner):
            level = group * SUB + inner
            upper = jnp.maximum(level - 1, 0)
            lower = jnp.minimum(level + 1, levels - 1)

            def column(c):
                center = qb[field, c, level, 8:24, :]
                near = qb[field, c, level, 7:23, :] + qb[field, c, level, 9:25, :]
                cross = near - 4.0 * center
                return (
                    center,
                    cross,
                    pltpu.roll(center, 2, 1),
                    pltpu.roll(center, LANES - 2, 1),
                    pltpu.roll(cross, 1, 1),
                    pltpu.roll(cross, LANES - 1, 1),
                )

            wrap = column(blocks)
            west, here = wrap, column(0)
            for c in range(blocks):
                east = column(c + 1) if c < blocks - 1 else wrap
                span = slice(c * LANES, (c + 1) * LANES)
                center, cross = here[0], here[1]
                far = qb[field, c, level, 6:22, :] + qb[field, c, level, 10:26, :]
                far = far + jnp.where(lane16 < 2, west[2], here[2])
                far = far + jnp.where(lane16 >= LANES - 2, east[3], here[3])
                near = jnp.where(lane16 < 1, west[4], here[4]) + jnp.where(
                    lane16 >= LANES - 1, east[5], here[5]
                )
                near = near - 4.0 * cross
                smooth = (near + near) + (far - 12.0 * center)
                both = qb[field, c, upper, 8:24, :] + qb[field, c, lower, 8:24, :]
                mixed = (0.6 * center + 0.2 * both) - betav[:, span] * smooth
                ocean_out[field, level, :, span] = mixed + turn * qb[partner, c, level, 8:24, :]
                west, here = here, east

        @pl.when((group == 0) & (field < 2))
        def _():
            for c in range(blocks):
                span = slice(c * LANES, (c + 1) * LANES)
                ocean_out[field, 0, :, span] = ocean_out[field, 0, :, span] + prevv[
                    jnp.minimum(field, 1), :, span
                ]

    @pl.loop(0, fields)
    def _(field):
        for way in range(3):
            edge_copies(edge_refs, field, way, edge_peers).wait_send()

        @pl.loop(0, groups)
        def _(group):
            for direction in range(2):
                copies(row_refs, direction, field, group, peers).wait_send()


def per_device(
    ocean_state,
    biharmonic,
    prev_stress,
    ice_state,
    strength,
    ice_mass,
    ice_fraction,
    wind_stress,
    ice_count,
    ice_list,
):
    fields, levels, rows, cols = ocean_state.shape
    blocks, groups = cols // LANES, levels // SUB
    f32 = jnp.float32
    dma = pltpu.SemaphoreType.DMA
    body = functools.partial(kernel, lax.axis_size("tile"), lax.axis_size("grp"))
    out_spec = pl.BlockSpec(memory_space=pltpu.VMEM)
    return pl.pallas_call(
        body,
        name="coupled",
        out_shape=OUT(ocean_state, ice_state, wind_stress),
        in_specs=[pl.BlockSpec(memory_space=pl.ANY)] * 8
        + [pl.BlockSpec(memory_space=pltpu.SMEM)] * 2,
        out_specs=[out_spec] * 3,
        scratch_shapes=[
            pltpu.VMEM((fields, blocks + 1, levels, SLAB, LANES), f32),
            pltpu.VMEM((rows, cols), f32),
            pltpu.VMEM((2, rows, cols), f32),
            pltpu.VMEM((12, blocks * rows, LANES), f32),
            pltpu.VMEM((5, rows, 2, SUB, LANES), f32),
            pltpu.VMEM((5, rows, 2, SUB, LANES), f32),
            pltpu.VMEM((2, fields, groups, 2, blocks, SUB, LANES), f32),
            pltpu.VMEM((2, fields, groups, 2, blocks, SUB, LANES), f32),
            pltpu.VMEM((fields, rows, LANES), f32),
            pltpu.VMEM((3, fields, rows, LANES), f32),
            dma((fields, blocks)),
            dma((2,)),
            dma((6, blocks)),
            dma((2, fields, groups)),
            dma((2, fields, groups)),
            dma((3, fields)),
            dma((3, fields)),
        ],
        compiler_params=pltpu.CompilerParams(
            collective_id=0, has_side_effects=True, vmem_limit_bytes=VLIM
        ),
    )(
        ocean_state,
        biharmonic,
        prev_stress,
        ice_state,
        strength,
        ice_mass,
        ice_fraction,
        wind_stress,
        ice_count,
        ice_list,
    )


VLIM = 58 << 20


def OUT(*arrays):
    return [jax.ShapeDtypeStruct(a.shape, a.dtype) for a in arrays]


def solution(mesh):
    wide = P(None, "tile", "grp")
    flat = P("tile", "grp")
    deep = P(None, None, "tile", "grp")
    return jax.shard_map(
        per_device,
        mesh=mesh,
        in_specs=(
            deep,
            flat,
            wide,
            wide,
            flat,
            flat,
            flat,
            wide,
            P(("grp", "tile")),
            P(("grp", "tile"), None),
        ),
        out_specs=(deep, wide, wide),
        check_vma=False,
    )
```

```python
import functools

import jax
import jax.numpy as jnp
from jax import lax
from jax.experimental import pallas as pl
from jax.experimental.pallas import tpu as pltpu
from jax.sharding import PartitionSpec as P

MESH = pl.DeviceIdType.MESH
LANES = 128
SUB = 8
SLAB = 32
SUBCYCLES = 64
THIRD = 2.0 / 3.0


def copies(refs, direction, field, group, peers):
    sbuf, rbuf, ssem, rsem = refs
    return pltpu.make_async_remote_copy(
        src_ref=sbuf.at[direction, field, group],
        dst_ref=rbuf.at[direction, field, group],
        send_sem=ssem.at[direction, field, group],
        recv_sem=rsem.at[direction, field, group],
        device_id=peers[direction],
        device_id_type=MESH,
    )


def edge_copies(refs, field, way, peers):
    esend, erecv, essem, ersem = refs
    return pltpu.make_async_remote_copy(
        src_ref=esend.at[field],
        dst_ref=erecv.at[way, field],
        send_sem=essem.at[way, field],
        recv_sem=ersem.at[way, field],
        device_id=peers[way],
        device_id_type=MESH,
    )


def kernel(
    n_tile,
    n_grp,
    ocean,
    beta,
    prev,
    ice,
    strength,
    mass,
    fraction,
    wind,
    count,
    listed,
    ocean_out,
    ice_out,
    stress_out,
    qb,
    betav,
    prevv,
    iceb,
    state,
    const,
    sbuf,
    rbuf,
    esend,
    erecv,
    qsem,
    bsem,
    isem,
    ssem,
    rsem,
    essem,
    ersem,
):
    fields, blocks, levels = ocean.shape[0], ocean.shape[3] // LANES, ocean.shape[1]
    groups = levels // SUB
    tile = lax.axis_index("tile")
    grp = lax.axis_index("grp")
    above = lax.rem(tile + 1, n_tile)
    below = lax.rem(tile + n_tile - 1, n_tile)
    other = lax.rem(grp + 1, n_grp)
    peers = [{"grp": grp, "tile": above}, {"grp": grp, "tile": below}]
    edge_peers = [
        {"grp": other, "tile": tile},
        {"grp": other, "tile": above},
        {"grp": other, "tile": below},
    ]
    row_refs = (sbuf, rbuf, ssem, rsem)
    edge_refs = (esend, erecv, essem, ersem)
    flat = qb.reshape(fields, blocks + 1, levels * SLAB, LANES)
    ice_view = iceb.reshape(12, blocks, 16, LANES)

    def columns(c):
        return pl.ds(pl.multiple_of(c * LANES, LANES), LANES)

    def load(field, c):
        return pltpu.make_async_copy(
            ocean.at[field, :, :, columns(c)], qb.at[field, c, :, 8:24, :], qsem.at[field, c]
        )

    def ice_loads(c):
        span = columns(c)
        pairs = [
            (ice.at[:, :, span], ice_view.at[0:5, c]),
            (strength.at[:, span], ice_view.at[5, c]),
            (mass.at[:, span], ice_view.at[6, c]),
            (fraction.at[:, span], ice_view.at[7, c]),
            (wind.at[:, :, span], ice_view.at[8:10, c]),
            (ocean.at[0:2, 0, :, span], ice_view.at[10:12, c]),
        ]
        return [pltpu.make_async_copy(s, d, isem.at[n, c]) for n, (s, d) in enumerate(pairs)]

    for field in range(fields):
        pl.loop(0, blocks)(lambda c, field=field: load(field, c).start())

    @pl.loop(0, blocks)
    def _(c):
        for copy in ice_loads(c):
            copy.start()

    beta_copy = pltpu.make_async_copy(beta, betav, bsem.at[0])
    prev_copy = pltpu.make_async_copy(prev, prevv, bsem.at[1])
    beta_copy.start()
    prev_copy.start()

    barrier = pltpu.get_barrier_semaphore()
    for peer in peers + edge_peers:
        pl.semaphore_signal(barrier, inc=1, device_id=peer, device_id_type=MESH)

    lane8 = lax.broadcasted_iota(jnp.int32, (SUB, LANES), 1)
    lane16 = lax.broadcasted_iota(jnp.int32, (2 * SUB, LANES), 1)
    for field in range(fields):
        pl.loop(0, blocks)(lambda c, field=field: load(field, c).wait())
        packed = jnp.zeros((2 * SUB, LANES), jnp.float32)
        for level in range(levels):
            ends = jnp.where(
                lane16 < 2, qb[field, 0, level, 8:24, :], qb[field, blocks - 1, level, 8:24, :]
            )
            ends = pltpu.roll(ends, 4 * level + 2, 1)
            packed = jnp.where(lane16 // 4 == level, ends, packed)
        esend[field] = packed
        for group in range(groups):
            first = SLAB * SUB * group + 8

            @pl.loop(0, blocks, unroll=True)
            def _(c):
                for row in range(2):
                    sbuf[0, field, group, row, c] = flat[
                        field, c, pl.ds(first + 14 + row, SUB, stride=SLAB), :
                    ]
                    sbuf[1, field, group, row, c] = flat[
                        field, c, pl.ds(first + row, SUB, stride=SLAB), :
                    ]

    pl.semaphore_wait(barrier, 5)
    for field in range(fields):
        for way in range(3):
            edge_copies(edge_refs, field, way, edge_peers).start()
        for group in range(groups):
            for direction in range(2):
                copies(row_refs, direction, field, group, peers).start()

    @pl.loop(0, blocks)
    def _(c):
        for copy in ice_loads(c):
            copy.wait()

    beta_copy.wait()
    prev_copy.wait()

    def ice_row(n, row):
        return jnp.stack(
            [iceb[n, pl.ds(LANES * half + row, SUB, stride=16), :] for half in range(2)]
        )

    for row in range(16):
        sxx, syy = ice_row(2, row), ice_row(3, row)
        state[0, row] = ice_row(0, row)
        state[1, row] = ice_row(1, row)
        state[2, row] = sxx + syy
        state[3, row] = 2.0 * (sxx - syy)
        state[4, row] = 4.0 * ice_row(4, row)
        m = ice_row(6, row)
        inverse = 1.0 / (m + 0.3)
        const[0, row] = (0.5 * THIRD) * ice_row(5, row)
        const[1, row] = m * inverse
        const[2, row] = 0.075 * inverse
        const[3, row] = 0.3 * inverse * (ice_row(8, row) + ice_row(10, row))
        const[4, row] = 0.3 * inverse * (ice_row(9, row) + ice_row(11, row))

    lane = lax.broadcasted_iota(jnp.int32, (2, SUB, LANES), 2)
    is_last = lane == LANES - 1
    is_first = lane == 0

    def ahead_x(q):
        return jnp.where(is_last, 0.0, pltpu.roll(q, LANES - 1, 2) - q)

    def behind_x(q):
        return q - jnp.where(is_first, 0.0, pltpu.roll(q, 1, 2))

    def subcycle():
        for row in range(16):
            u, v = state[0, row], state[1, row]
            du_dx, dv_dx = ahead_x(u), ahead_x(v)
            if row < 15:
                du_dy, dv_dy = state[0, row + 1] - u, state[1, row + 1] - v
                div, ten, shr = du_dx + dv_dy, du_dx - dv_dy, du_dy + dv_dx
            else:
                div, ten, shr = du_dx, du_dx, dv_dx
            twice = div + div
            root = lax.rsqrt(twice * twice + ten * ten + shr * shr + 1.0)
            pressure = const[0, row]
            scaled = pressure * root
            state[2, row] = THIRD * state[2, row] + (scaled * twice - pressure)
            state[3, row] = THIRD * state[3, row] + scaled * ten
            state[4, row] = THIRD * state[4, row] + scaled * shr
        before_yy = None
        for row in range(16):
            one, two, xy = state[2, row], state[3, row], state[4, row]
            one = one + one
            xx, yy = one + two, one - two
            force_x, force_y = behind_x(xx), behind_x(xy)
            if row:
                force_x, force_y = force_x + (xy - state[4, row - 1]), force_y + (yy - before_yy)
            else:
                force_x, force_y = force_x + xy, force_y + yy
            before_yy = yy
            keep, push = const[1, row], const[2, row]
            u, v = state[0, row], state[1, row]
            state[0, row] = keep * (u + 0.09 * v) + (const[3, row] + push * force_x)
            state[1, row] = keep * (v - 0.09 * u) + (const[4, row] + push * force_y)

    @pl.loop(0, SUBCYCLES, step=2)
    def _(step):
        subcycle()
        subcycle()

    number = lax.broadcasted_iota(jnp.int32, (2, SUB, LANES), 0) * SUB + lax.broadcasted_iota(
        jnp.int32, (2, SUB, LANES), 1
    )
    covered = jnp.zeros((2, SUB, LANES), jnp.int32)
    for slot in range(blocks):
        block = jnp.where(slot < count[0], listed[0, slot], -1)
        covered = jnp.where(number == block, 1, covered)
    covered = covered > 0
    for row in range(16):
        u, v = state[0, row], state[1, row]
        one, two, xy = state[2, row], state[3, row], state[4, row]
        part = ice_row(7, row)
        results = {
            0: u,
            1: v,
            2: 0.5 * one + 0.25 * two,
            3: 0.5 * one - 0.25 * two,
            4: 0.25 * xy,
            8: part * (u - ice_row(10, row)) + (1.0 - part) * ice_row(8, row),
            9: part * (v - ice_row(11, row)) + (1.0 - part) * ice_row(9, row),
        }
        for n, result in results.items():
            result = jnp.where(covered, result, ice_row(n, row))
            for half in range(2):
                iceb[n, pl.ds(LANES * half + row, SUB, stride=16), :] = result[half]
    for c in range(blocks):
        span = slice(c * LANES, (c + 1) * LANES)
        for n in range(5):
            ice_out[n, :, span] = ice_view[n, c]
        for n in range(2):
            stress_out[n, :, span] = ice_view[8 + n, c]

    has_below = tile > 0
    has_above = tile < n_tile - 1
    place = (tile * 16).astype(jnp.float32) + 0.5
    place = place + lax.broadcasted_iota(jnp.int32, (16, LANES), 0).astype(jnp.float32)
    coriolis = 0.2 * (2.0 * place / (16.0 * n_tile) - 1.0)

    def masked(flag, x):
        return jnp.where(flag, x, jnp.zeros_like(x))

    @pl.loop(0, fields * groups)
    def _(chunk):
        field = lax.div(chunk, groups)
        group = lax.rem(chunk, groups)

        @pl.when(group == 0)
        def _():
            for way in range(3):
                edge_copies(edge_refs, field, way, edge_peers).wait_recv()

        for direction in range(2):
            copies(row_refs, direction, field, group, peers).wait_recv()

        @pl.loop(0, blocks, unroll=True)
        def _(c):
            first = pl.multiple_of(SLAB * SUB * group, SUB)
            for row in range(2):
                flat[field, c, pl.ds(first + 6 + row, SUB, stride=SLAB), :] = masked(
                    has_below, rbuf[0, field, group, row, c]
                )
                flat[field, c, pl.ds(first + 24 + row, SUB, stride=SLAB), :] = masked(
                    has_above, rbuf[1, field, group, row, c]
                )

        for inner in range(SUB):
            level = group * SUB + inner
            shift = lax.rem(2 * LANES - 2 - 4 * level, LANES)
            qb[field, blocks, level, 8:24, :] = pltpu.roll(erecv[0, field], shift, 1)
            qb[field, blocks, level, 0:8, :] = masked(
                has_below, pltpu.roll(erecv[1, field, 8:16], shift, 1)
            )
            qb[field, blocks, level, 24:32, :] = masked(
                has_above, pltpu.roll(erecv[2, field, 0:8], shift, 1)
            )

        turn = jnp.where(field == 0, 1.0, jnp.where(field == 1, -1.0, 0.0)) * coriolis
        partner = jnp.where(field == 0, 1, 0)

        for inner in range(SUB):
            level = group * SUB + inner
            upper = jnp.maximum(level - 1, 0)
            lower = jnp.minimum(level + 1, levels - 1)

            def column(c):
                center = qb[field, c, level, 8:24, :]
                near = qb[field, c, level, 7:23, :] + qb[field, c, level, 9:25, :]
                cross = near - 4.0 * center
                return (
                    center,
                    cross,
                    pltpu.roll(center, 2, 1),
                    pltpu.roll(center, LANES - 2, 1),
                    pltpu.roll(cross, 1, 1),
                    pltpu.roll(cross, LANES - 1, 1),
                )

            wrap = column(blocks)
            west, here = wrap, column(0)
            for c in range(blocks):
                east = column(c + 1) if c < blocks - 1 else wrap
                span = slice(c * LANES, (c + 1) * LANES)
                center, cross = here[0], here[1]
                far = qb[field, c, level, 6:22, :] + qb[field, c, level, 10:26, :]
                far = far + jnp.where(lane16 < 2, west[2], here[2])
                far = far + jnp.where(lane16 >= LANES - 2, east[3], here[3])
                near = jnp.where(lane16 < 1, west[4], here[4]) + jnp.where(
                    lane16 >= LANES - 1, east[5], here[5]
                )
                near = near - 4.0 * cross
                smooth = (near + near) + (far - 12.0 * center)
                both = qb[field, c, upper, 8:24, :] + qb[field, c, lower, 8:24, :]
                mixed = (0.6 * center + 0.2 * both) - betav[:, span] * smooth
                ocean_out[field, level, :, span] = mixed + turn * qb[partner, c, level, 8:24, :]
                west, here = here, east

        @pl.when((group == 0) & (field < 2))
        def _():
            for c in range(blocks):
                span = slice(c * LANES, (c + 1) * LANES)
                ocean_out[field, 0, :, span] = ocean_out[field, 0, :, span] + prevv[
                    jnp.minimum(field, 1), :, span
                ]

    @pl.loop(0, fields)
    def _(field):
        for way in range(3):
            edge_copies(edge_refs, field, way, edge_peers).wait_send()

        @pl.loop(0, groups)
        def _(group):
            for direction in range(2):
                copies(row_refs, direction, field, group, peers).wait_send()


def per_device(
    ocean_state,
    biharmonic,
    prev_stress,
    ice_state,
    strength,
    ice_mass,
    ice_fraction,
    wind_stress,
    ice_count,
    ice_list,
):
    fields, levels, rows, cols = ocean_state.shape
    blocks, groups = cols // LANES, levels // SUB
    f32 = jnp.float32
    dma = pltpu.SemaphoreType.DMA
    body = functools.partial(kernel, lax.axis_size("tile"), lax.axis_size("grp"))
    out_spec = pl.BlockSpec(memory_space=pltpu.VMEM)
    return pl.pallas_call(
        body,
        name="coupled",
        out_shape=[pltpu.VMEM(a.shape, a.dtype) for a in (ocean_state, ice_state, wind_stress)],
        in_specs=[pl.BlockSpec(memory_space=pltpu.HBM)] * 8
        + [pl.BlockSpec(memory_space=pltpu.SMEM)] * 2,
        out_specs=[out_spec] * 3,
        scratch_shapes=[
            pltpu.VMEM((fields, blocks + 1, levels, SLAB, LANES), f32),
            pltpu.VMEM((rows, cols), f32),
            pltpu.VMEM((2, rows, cols), f32),
            pltpu.VMEM((12, blocks * rows, LANES), f32),
            pltpu.VMEM((5, rows, 2, SUB, LANES), f32),
            pltpu.VMEM((5, rows, 2, SUB, LANES), f32),
            pltpu.VMEM((2, fields, groups, 2, blocks, SUB, LANES), f32),
            pltpu.VMEM((2, fields, groups, 2, blocks, SUB, LANES), f32),
            pltpu.VMEM((fields, rows, LANES), f32),
            pltpu.VMEM((3, fields, rows, LANES), f32),
            dma((fields, blocks)),
            dma((2,)),
            dma((6, blocks)),
            dma((2, fields, groups)),
            dma((2, fields, groups)),
            dma((3, fields)),
            dma((3, fields)),
        ],
        compiler_params=pltpu.CompilerParams(
            collective_id=0, has_side_effects=True, vmem_limit_bytes=44 << 20
        ),
    )(
        ocean_state,
        biharmonic,
        prev_stress,
        ice_state,
        strength,
        ice_mass,
        ice_fraction,
        wind_stress,
        ice_count,
        ice_list,
    )


def solution(mesh):
    wide = P(None, "tile", "grp")
    flat = P("tile", "grp")
    deep = P(None, None, "tile", "grp")
    return jax.shard_map(
        per_device,
        mesh=mesh,
        in_specs=(
            deep,
            flat,
            wide,
            wide,
            flat,
            flat,
            flat,
            wide,
            P(("grp", "tile")),
            P(("grp", "tile"), None),
        ),
        out_specs=(deep, wide, wide),
        check_vma=False,
    )
```

```python
import functools

import jax
import jax.numpy as jnp
from jax import lax
from jax.experimental import pallas as pl
from jax.experimental.pallas import tpu as pltpu
from jax.sharding import PartitionSpec as P

MESH = pl.DeviceIdType.MESH
LANES = 128
SUB = 8
SLAB = 32
SUBCYCLES = 64
BEFORE_PACK = 4
BEFORE_FIRST_ROW = 24
THIRD = 2.0 / 3.0


def copies(refs, direction, field, group, peers):
    sbuf, rbuf, ssem, rsem = refs
    return pltpu.make_async_remote_copy(
        src_ref=sbuf.at[direction, field, group],
        dst_ref=rbuf.at[direction, field, group],
        send_sem=ssem.at[direction, field, group],
        recv_sem=rsem.at[direction, field, group],
        device_id=peers[direction],
        device_id_type=MESH,
    )


def edge_copies(refs, field, way, peers):
    esend, erecv, essem, ersem = refs
    return pltpu.make_async_remote_copy(
        src_ref=esend.at[field],
        dst_ref=erecv.at[way, field],
        send_sem=essem.at[way, field],
        recv_sem=ersem.at[way, field],
        device_id=peers[way],
        device_id_type=MESH,
    )


def kernel(
    n_tile,
    n_grp,
    ocean,
    beta,
    prev,
    ice,
    strength,
    mass,
    fraction,
    wind,
    count,
    listed,
    ocean_out,
    ice_out,
    stress_out,
    qb,
    betav,
    prevv,
    iceb,
    state,
    const,
    sbuf,
    rbuf,
    esend,
    erecv,
    qsem,
    bsem,
    isem,
    ssem,
    rsem,
    essem,
    ersem,
):
    fields, blocks, levels = ocean.shape[0], ocean.shape[3] // LANES, ocean.shape[1]
    groups = levels // SUB
    tile = lax.axis_index("tile")
    grp = lax.axis_index("grp")
    above = lax.rem(tile + 1, n_tile)
    below = lax.rem(tile + n_tile - 1, n_tile)
    other = lax.rem(grp + 1, n_grp)
    peers = [{"grp": grp, "tile": above}, {"grp": grp, "tile": below}]
    edge_peers = [
        {"grp": other, "tile": tile},
        {"grp": other, "tile": above},
        {"grp": other, "tile": below},
    ]
    row_refs = (sbuf, rbuf, ssem, rsem)
    edge_refs = (esend, erecv, essem, ersem)
    flat = qb.reshape(fields, blocks + 1, levels * SLAB, LANES)
    ice_view = iceb.reshape(12, blocks, 16, LANES)

    def columns(c):
        return pl.ds(pl.multiple_of(c * LANES, LANES), LANES)

    def load(field, c):
        return pltpu.make_async_copy(
            ocean.at[field, :, :, columns(c)], qb.at[field, c, :, 8:24, :], qsem.at[field, c]
        )

    def ice_loads(c):
        span = columns(c)
        pairs = [
            (ice.at[:, :, span], ice_view.at[0:5, c]),
            (strength.at[:, span], ice_view.at[5, c]),
            (mass.at[:, span], ice_view.at[6, c]),
            (fraction.at[:, span], ice_view.at[7, c]),
            (wind.at[:, :, span], ice_view.at[8:10, c]),
            (ocean.at[0:2, 0, :, span], ice_view.at[10:12, c]),
        ]
        return [pltpu.make_async_copy(s, d, isem.at[n, c]) for n, (s, d) in enumerate(pairs)]

    @pl.loop(0, blocks)
    def _(c):
        for copy in ice_loads(c):
            copy.start()

    for field in range(fields):
        pl.loop(0, blocks)(lambda c, field=field: load(field, c).start())

    beta_copy = pltpu.make_async_copy(beta, betav, bsem.at[0])
    prev_copy = pltpu.make_async_copy(prev, prevv, bsem.at[1])
    beta_copy.start()
    prev_copy.start()

    has_below = tile > 0
    has_above = tile < n_tile - 1
    always = tile >= 0
    sends = [has_above, has_below]
    receives = [has_below, has_above]
    edge_sends = [always, has_above, has_below]
    edge_receives = [always, has_below, has_above]

    barrier = pltpu.get_barrier_semaphore()
    for peer, exists in zip(peers + edge_peers, sends + edge_sends):

        @pl.when(exists)
        def _(peer=peer):
            pl.semaphore_signal(barrier, inc=1, device_id=peer, device_id_type=MESH)

    lane16 = lax.broadcasted_iota(jnp.int32, (2 * SUB, LANES), 1)
    def exchange():
        pl.when(has_below & has_above)(lambda: pl.semaphore_wait(barrier, 5))
        pl.when(jnp.logical_not(has_below & has_above))(lambda: pl.semaphore_wait(barrier, 3))
        for field in range(fields):
            for way in range(3):
                pl.when(edge_sends[way])(
                    lambda field=field, way=way: edge_copies(
                        edge_refs, field, way, edge_peers
                    ).start()
                )
            for group in range(groups):
                for direction in range(2):
                    pl.when(sends[direction])(
                        lambda field=field, group=group, direction=direction: copies(
                            row_refs, direction, field, group, peers
                        ).start()
                    )

    @pl.loop(0, blocks)
    def _(c):
        for copy in ice_loads(c):
            copy.wait()

    def ice_row(n, row):
        return jnp.stack(
            [iceb[n, pl.ds(LANES * half + row, SUB, stride=16), :] for half in range(2)]
        )

    for row in range(16):
        sxx, syy = ice_row(2, row), ice_row(3, row)
        state[0, row] = ice_row(0, row)
        state[1, row] = ice_row(1, row)
        state[2, row] = sxx + syy
        state[3, row] = 2.0 * (sxx - syy)
        state[4, row] = 4.0 * ice_row(4, row)
        m = ice_row(6, row)
        inverse = 1.0 / (m + 0.3)
        const[0, row] = (0.5 * THIRD) * ice_row(5, row)
        const[1, row] = m * inverse
        const[2, row] = 0.075 * inverse
        const[3, row] = 0.3 * inverse * (ice_row(8, row) + ice_row(10, row))
        const[4, row] = 0.3 * inverse * (ice_row(9, row) + ice_row(11, row))

    lane = lax.broadcasted_iota(jnp.int32, (2, SUB, LANES), 2)
    is_last = lane == LANES - 1
    is_first = lane == 0

    def ahead_x(q):
        return jnp.where(is_last, 0.0, pltpu.roll(q, LANES - 1, 2) - q)

    def behind_x(q):
        return q - jnp.where(is_first, 0.0, pltpu.roll(q, 1, 2))

    def subcycle():
        for row in range(16):
            u, v = state[0, row], state[1, row]
            du_dx, dv_dx = ahead_x(u), ahead_x(v)
            if row < 15:
                du_dy, dv_dy = state[0, row + 1] - u, state[1, row + 1] - v
                div, ten, shr = du_dx + dv_dy, du_dx - dv_dy, du_dy + dv_dx
            else:
                div, ten, shr = du_dx, du_dx, dv_dx
            twice = div + div
            root = lax.rsqrt(twice * twice + ten * ten + shr * shr + 1.0)
            pressure = const[0, row]
            scaled = pressure * root
            state[2, row] = THIRD * state[2, row] + (scaled * twice - pressure)
            state[3, row] = THIRD * state[3, row] + scaled * ten
            state[4, row] = THIRD * state[4, row] + scaled * shr
        before_yy = None
        for row in range(16):
            one, two, xy = state[2, row], state[3, row], state[4, row]
            one = one + one
            xx, yy = one + two, one - two
            force_x, force_y = behind_x(xx), behind_x(xy)
            if row:
                force_x, force_y = force_x + (xy - state[4, row - 1]), force_y + (yy - before_yy)
            else:
                force_x, force_y = force_x + xy, force_y + yy
            before_yy = yy
            keep, push = const[1, row], const[2, row]
            u, v = state[0, row], state[1, row]
            state[0, row] = keep * (u + 0.09 * v) + (const[3, row] + push * force_x)
            state[1, row] = keep * (v - 0.09 * u) + (const[4, row] + push * force_y)

    def subcycles(first, last):
        @pl.loop(first, last, step=2)
        def _(step):
            subcycle()
            subcycle()

    subcycles(0, BEFORE_PACK)
    for field in range(fields):
        pl.loop(0, blocks)(lambda c, field=field: load(field, c).wait())
        packed = jnp.zeros((2 * SUB, LANES), jnp.float32)
        for level in range(levels):
            ends = jnp.where(
                lane16 < 2, qb[field, 0, level, 8:24, :], qb[field, blocks - 1, level, 8:24, :]
            )
            ends = pltpu.roll(ends, 4 * level + 2, 1)
            packed = jnp.where(lane16 // 4 == level, ends, packed)
        esend[field] = packed
        for group in range(groups):
            first = SLAB * SUB * group + 8

            @pl.loop(0, blocks, unroll=True)
            def _(c):
                for row in range(2):
                    sbuf[0, field, group, row, c] = flat[
                        field, c, pl.ds(first + 14 + row, SUB, stride=SLAB), :
                    ]
                    sbuf[1, field, group, row, c] = flat[
                        field, c, pl.ds(first + row, SUB, stride=SLAB), :
                    ]

    pl.when(has_below)(exchange)
    subcycles(BEFORE_PACK, BEFORE_FIRST_ROW)
    pl.when(jnp.logical_not(has_below))(exchange)
    subcycles(BEFORE_FIRST_ROW, SUBCYCLES)
    beta_copy.wait()
    prev_copy.wait()

    number = lax.broadcasted_iota(jnp.int32, (2, SUB, LANES), 0) * SUB + lax.broadcasted_iota(
        jnp.int32, (2, SUB, LANES), 1
    )
    covered = jnp.zeros((2, SUB, LANES), jnp.int32)
    for slot in range(blocks):
        block = jnp.where(slot < count[0], listed[slot], -1)
        covered = jnp.where(number == block, 1, covered)
    covered = covered > 0
    for row in range(16):
        u, v = state[0, row], state[1, row]
        one, two, xy = state[2, row], state[3, row], state[4, row]
        part = ice_row(7, row)
        results = {
            0: u,
            1: v,
            2: 0.5 * one + 0.25 * two,
            3: 0.5 * one - 0.25 * two,
            4: 0.25 * xy,
            8: part * (u - ice_row(10, row)) + (1.0 - part) * ice_row(8, row),
            9: part * (v - ice_row(11, row)) + (1.0 - part) * ice_row(9, row),
        }
        for n, result in results.items():
            result = jnp.where(covered, result, ice_row(n, row))
            for half in range(2):
                iceb[n, pl.ds(LANES * half + row, SUB, stride=16), :] = result[half]
    for c in range(blocks):
        span = slice(c * LANES, (c + 1) * LANES)
        for n in range(5):
            ice_out[n, :, span] = ice_view[n, c]
        for n in range(2):
            stress_out[n, :, span] = ice_view[8 + n, c]

    place = (tile * 16).astype(jnp.float32) + 0.5
    place = place + lax.broadcasted_iota(jnp.int32, (16, LANES), 0).astype(jnp.float32)
    coriolis = 0.2 * (2.0 * place / (16.0 * n_tile) - 1.0)

    @pl.loop(0, fields * groups)
    def _(chunk):
        field = lax.div(chunk, groups)
        group = lax.rem(chunk, groups)

        @pl.when(group == 0)
        def _():
            for way in range(3):
                pl.when(edge_receives[way])(
                    lambda way=way: edge_copies(edge_refs, field, way, edge_peers).wait_recv()
                )

        first = pl.multiple_of(SLAB * SUB * group, SUB)

        def shifted(inner, x):
            return pltpu.roll(x, lax.rem(2 * LANES - 2 - 4 * (group * SUB + inner), LANES), 1)

        for direction, offset, corner in ((0, 6, 0), (1, 24, 24)):
            part = erecv.at[1, field, 8:16] if direction == 0 else erecv.at[2, field, 0:8]

            @pl.when(receives[direction])
            def _(direction=direction, offset=offset, corner=corner, part=part):
                copies(row_refs, direction, field, group, peers).wait_recv()

                @pl.loop(0, blocks, unroll=True)
                def _(c):
                    for row in range(2):
                        flat[field, c, pl.ds(first + offset + row, SUB, stride=SLAB), :] = rbuf[
                            direction, field, group, row, c
                        ]

                for inner in range(SUB):
                    qb[field, blocks, group * SUB + inner, corner : corner + 8, :] = shifted(
                        inner, part[...]
                    )

            @pl.when(jnp.logical_not(receives[direction]))
            def _(offset=offset):
                @pl.loop(0, blocks + 1)
                def _(c):
                    for row in range(2):
                        flat[field, c, pl.ds(first + offset + row, SUB, stride=SLAB), :] = (
                            jnp.zeros((SUB, LANES), jnp.float32)
                        )

        for inner in range(SUB):
            qb[field, blocks, group * SUB + inner, 8:24, :] = shifted(inner, erecv[0, field])

        turn = jnp.where(field == 0, 1.0, jnp.where(field == 1, -1.0, 0.0)) * coriolis
        partner = jnp.where(field == 0, 1, 0)

        for inner in range(SUB):
            level = group * SUB + inner
            upper = jnp.maximum(level - 1, 0)
            lower = jnp.minimum(level + 1, levels - 1)

            def column(c):
                center = qb[field, c, level, 8:24, :]
                near = qb[field, c, level, 7:23, :] + qb[field, c, level, 9:25, :]
                cross = near - 4.0 * center
                return (
                    center,
                    cross,
                    pltpu.roll(center, 2, 1),
                    pltpu.roll(center, LANES - 2, 1),
                    pltpu.roll(cross, 1, 1),
                    pltpu.roll(cross, LANES - 1, 1),
                )

            wrap = column(blocks)
            west, here = wrap, column(0)
            for c in range(blocks):
                east = column(c + 1) if c < blocks - 1 else wrap
                span = slice(c * LANES, (c + 1) * LANES)
                center, cross = here[0], here[1]
                far = qb[field, c, level, 6:22, :] + qb[field, c, level, 10:26, :]
                far = far + jnp.where(lane16 < 2, west[2], here[2])
                far = far + jnp.where(lane16 >= LANES - 2, east[3], here[3])
                near = jnp.where(lane16 < 1, west[4], here[4]) + jnp.where(
                    lane16 >= LANES - 1, east[5], here[5]
                )
                near = near - 4.0 * cross
                smooth = (near + near) + (far - 12.0 * center)
                both = qb[field, c, upper, 8:24, :] + qb[field, c, lower, 8:24, :]
                mixed = (0.6 * center + 0.2 * both) - betav[:, span] * smooth
                ocean_out[field, level, :, span] = mixed + turn * qb[partner, c, level, 8:24, :]
                west, here = here, east

        @pl.when((group == 0) & (field < 2))
        def _():
            for c in range(blocks):
                span = slice(c * LANES, (c + 1) * LANES)
                ocean_out[field, 0, :, span] = ocean_out[field, 0, :, span] + prevv[
                    jnp.minimum(field, 1), :, span
                ]

    @pl.loop(0, fields)
    def _(field):
        for way in range(3):
            pl.when(edge_sends[way])(
                lambda way=way: edge_copies(edge_refs, field, way, edge_peers).wait_send()
            )

        @pl.loop(0, groups)
        def _(group):
            for direction in range(2):
                pl.when(sends[direction])(
                    lambda direction=direction: copies(
                        row_refs, direction, field, group, peers
                    ).wait_send()
                )


def store_kernel(ocean, ice, stress, ocean_out, ice_out, stress_out, sem):
    pieces = [(ice, ice_out), (stress, stress_out)]
    for field in range(ocean.shape[0]):
        for half in range(2):
            span = pl.ds(half * (ocean.shape[1] // 2), ocean.shape[1] // 2)
            pieces.append((ocean.at[field, span], ocean_out.at[field, span]))
    started = [pltpu.make_async_copy(a, b, sem.at[n]) for n, (a, b) in enumerate(pieces)]
    for copy in started:
        copy.start()
    for copy in started:
        copy.wait()


def per_device(
    ocean_state,
    biharmonic,
    prev_stress,
    ice_state,
    strength,
    ice_mass,
    ice_fraction,
    wind_stress,
    ice_count,
    ice_list,
):
    fields, levels, rows, cols = ocean_state.shape
    blocks, groups = cols // LANES, levels // SUB
    f32 = jnp.float32
    dma = pltpu.SemaphoreType.DMA
    body = functools.partial(kernel, lax.axis_size("tile"), lax.axis_size("grp"))
    out_spec = pl.BlockSpec(memory_space=pltpu.VMEM)
    held = pl.pallas_call(
        body,
        name="coupled",
        out_shape=[pltpu.VMEM(a.shape, a.dtype) for a in (ocean_state, ice_state, wind_stress)],
        in_specs=[pl.BlockSpec(memory_space=pltpu.HBM)] * 8
        + [pl.BlockSpec(memory_space=pltpu.SMEM)] * 2,
        out_specs=[out_spec] * 3,
        scratch_shapes=[
            pltpu.VMEM((fields, blocks + 1, levels, SLAB, LANES), f32),
            pltpu.VMEM((rows, cols), f32),
            pltpu.VMEM((2, rows, cols), f32),
            pltpu.VMEM((12, blocks * rows, LANES), f32),
            pltpu.VMEM((5, rows, 2, SUB, LANES), f32),
            pltpu.VMEM((5, rows, 2, SUB, LANES), f32),
            pltpu.VMEM((2, fields, groups, 2, blocks, SUB, LANES), f32),
            pltpu.VMEM((2, fields, groups, 2, blocks, SUB, LANES), f32),
            pltpu.VMEM((fields, rows, LANES), f32),
            pltpu.VMEM((3, fields, rows, LANES), f32),
            dma((fields, blocks)),
            dma((2,)),
            dma((6, blocks)),
            dma((2, fields, groups)),
            dma((2, fields, groups)),
            dma((3, fields)),
            dma((3, fields)),
        ],
        compiler_params=pltpu.CompilerParams(
            collective_id=0, has_side_effects=True, vmem_limit_bytes=44 << 20
        ),
    )(
        ocean_state,
        biharmonic,
        prev_stress,
        ice_state,
        strength,
        ice_mass,
        ice_fraction,
        wind_stress,
        ice_count,
        ice_list.reshape(-1),
    )
    return pl.pallas_call(
        store_kernel,
        name="store",
        out_shape=[
            jax.ShapeDtypeStruct(a.shape, a.dtype) for a in (ocean_state, ice_state, wind_stress)
        ],
        in_specs=[pl.BlockSpec(memory_space=pltpu.VMEM)] * 3,
        out_specs=[pl.BlockSpec(memory_space=pltpu.HBM)] * 3,
        scratch_shapes=[dma((2 + 2 * fields,))],
        compiler_params=pltpu.CompilerParams(vmem_limit_bytes=14 << 20),
    )(*[pltpu.with_memory_space_constraint(array, pltpu.VMEM) for array in held])


def solution(mesh):
    wide = P(None, "tile", "grp")
    flat = P("tile", "grp")
    deep = P(None, None, "tile", "grp")
    return jax.shard_map(
        per_device,
        mesh=mesh,
        in_specs=(
            deep,
            flat,
            wide,
            wide,
            flat,
            flat,
            flat,
            wide,
            P(("grp", "tile")),
            P(("grp", "tile"), None),
        ),
        out_specs=(deep, wide, wide),
        check_vma=False,
    )
```

```python
import functools

import jax
import jax.numpy as jnp
from jax import lax
from jax.experimental import pallas as pl
from jax.experimental.pallas import tpu as pltpu
from jax.sharding import PartitionSpec as P

MESH = pl.DeviceIdType.MESH
LANES = 128
SUB = 8
SLAB = 32
SUBCYCLES = 64
BEFORE_PACK = 2
KERNEL_LIMIT = 35 << 20
FINISH_LIMIT = 8 << 20
BEFORE_FIRST_ROW = 24
THIRD = 2.0 / 3.0


def copies(refs, direction, field, group, peers):
    sbuf, rbuf, ssem, rsem = refs
    return pltpu.make_async_remote_copy(
        src_ref=sbuf.at[direction, field, group],
        dst_ref=rbuf.at[direction, field, group],
        send_sem=ssem.at[direction, field, group],
        recv_sem=rsem.at[direction, field, group],
        device_id=peers[direction],
        device_id_type=MESH,
    )


def edge_copies(refs, field, way, peers):
    esend, erecv, essem, ersem = refs
    return pltpu.make_async_remote_copy(
        src_ref=esend.at[field],
        dst_ref=erecv.at[way, field],
        send_sem=essem.at[way, field],
        recv_sem=ersem.at[way, field],
        device_id=peers[way],
        device_id_type=MESH,
    )


def ocean_level(q, betav, level, emit):
    blocks, levels = q.shape[0] - 1, q.shape[1]
    lane = lax.broadcasted_iota(jnp.int32, (2 * SUB, LANES), 1)
    upper = jnp.maximum(level - 1, 0)
    lower = jnp.minimum(level + 1, levels - 1)

    def column(c):
        center = q[c, level, 8:24, :]
        near = q[c, level, 7:23, :] + q[c, level, 9:25, :]
        cross = near - 4.0 * center
        return (
            center,
            cross,
            pltpu.roll(center, 2, 1),
            pltpu.roll(center, LANES - 2, 1),
            pltpu.roll(cross, 1, 1),
            pltpu.roll(cross, LANES - 1, 1),
        )

    wrap = column(blocks)
    west, here = wrap, column(0)
    for c in range(blocks):
        east = column(c + 1) if c < blocks - 1 else wrap
        span = slice(c * LANES, (c + 1) * LANES)
        center, cross = here[0], here[1]
        far = q[c, level, 6:22, :] + q[c, level, 10:26, :]
        far = far + jnp.where(lane < 2, west[2], here[2])
        far = far + jnp.where(lane >= LANES - 2, east[3], here[3])
        near = jnp.where(lane < 1, west[4], here[4]) + jnp.where(
            lane >= LANES - 1, east[5], here[5]
        )
        near = near - 4.0 * cross
        smooth = (near + near) + (far - 12.0 * center)
        both = q[c, upper, 8:24, :] + q[c, lower, 8:24, :]
        emit(c, span, (0.6 * center + 0.2 * both) - betav[:, span] * smooth)
        west, here = here, east


def kernel(
    n_tile,
    n_grp,
    ocean,
    beta,
    prev,
    ice,
    strength,
    mass,
    fraction,
    wind,
    count,
    listed_hbm,
    ocean_out,
    ice_out,
    stress_out,
    qb,
    betav,
    listed,
    prevv,
    iceb,
    state,
    const,
    sbuf,
    rbuf,
    esend,
    erecv,
    qsem,
    bsem,
    isem,
    ssem,
    rsem,
    essem,
    ersem,
):
    fields, blocks, levels = ocean.shape[0], ocean.shape[3] // LANES, ocean.shape[1]
    groups = levels // SUB
    tile = lax.axis_index("tile")
    grp = lax.axis_index("grp")
    above = lax.rem(tile + 1, n_tile)
    below = lax.rem(tile + n_tile - 1, n_tile)
    other = lax.rem(grp + 1, n_grp)
    peers = [{"grp": grp, "tile": above}, {"grp": grp, "tile": below}]
    edge_peers = [
        {"grp": other, "tile": tile},
        {"grp": other, "tile": above},
        {"grp": other, "tile": below},
    ]
    row_refs = (sbuf, rbuf, ssem, rsem)
    edge_refs = (esend, erecv, essem, ersem)
    flat = qb.reshape(fields, blocks + 1, levels * SLAB, LANES)
    ice_view = iceb.reshape(12, blocks, 16, LANES)

    def columns(c):
        return pl.ds(pl.multiple_of(c * LANES, LANES), LANES)

    def load(field, c):
        return pltpu.make_async_copy(
            ocean.at[field, :, :, columns(c)], qb.at[field, c, :, 8:24, :], qsem.at[field, c]
        )

    def ice_loads(c):
        span = columns(c)
        pairs = [
            (ice.at[:, :, span], ice_view.at[0:5, c]),
            (strength.at[:, span], ice_view.at[5, c]),
            (mass.at[:, span], ice_view.at[6, c]),
            (fraction.at[:, span], ice_view.at[7, c]),
            (wind.at[:, :, span], ice_view.at[8:10, c]),
            (ocean.at[0:2, 0, :, span], ice_view.at[10:12, c]),
        ]
        return [pltpu.make_async_copy(s, d, isem.at[n, c]) for n, (s, d) in enumerate(pairs)]

    @pl.loop(0, blocks)
    def _(c):
        for copy in ice_loads(c):
            copy.start()

    for field in range(fields):
        pl.loop(0, blocks)(lambda c, field=field: load(field, c).start())

    beta_copy = pltpu.make_async_copy(beta, betav, bsem.at[0])
    prev_copy = pltpu.make_async_copy(prev, prevv, bsem.at[1])
    list_copy = pltpu.make_async_copy(listed_hbm, listed, bsem.at[2])
    list_copy.start()
    beta_copy.start()
    prev_copy.start()

    has_below = tile > 0
    has_above = tile < n_tile - 1
    always = tile >= 0
    sends = [has_above, has_below]
    receives = [has_below, has_above]
    edge_sends = [always, has_above, has_below]
    edge_receives = [always, has_below, has_above]

    barrier = pltpu.get_barrier_semaphore()
    for peer, exists in zip(peers + edge_peers, sends + edge_sends):

        @pl.when(exists)
        def _(peer=peer):
            pl.semaphore_signal(barrier, inc=1, device_id=peer, device_id_type=MESH)

    lane16 = lax.broadcasted_iota(jnp.int32, (2 * SUB, LANES), 1)
    def meet():
        pl.when(has_below & has_above)(lambda: pl.semaphore_wait(barrier, 5))
        pl.when(jnp.logical_not(has_below & has_above))(lambda: pl.semaphore_wait(barrier, 3))

    def send(field):
        for way in range(3):
            pl.when(edge_sends[way])(
                lambda way=way: edge_copies(edge_refs, field, way, edge_peers).start()
            )
        for group in range(groups):
            for direction in range(2):
                pl.when(sends[direction])(
                    lambda group=group, direction=direction: copies(
                        row_refs, direction, field, group, peers
                    ).start()
                )

    def exchange():
        meet()
        for field in range(fields):
            send(field)

    @pl.loop(0, blocks)
    def _(c):
        for copy in ice_loads(c):
            copy.wait()

    def ice_row(n, row):
        return jnp.stack(
            [iceb[n, pl.ds(LANES * half + row, SUB, stride=16), :] for half in range(2)]
        )

    for row in range(16):
        sxx, syy = ice_row(2, row), ice_row(3, row)
        state[0, row] = ice_row(0, row)
        state[1, row] = ice_row(1, row)
        state[2, row] = sxx + syy
        state[3, row] = 2.0 * (sxx - syy)
        state[4, row] = 4.0 * ice_row(4, row)
        m = ice_row(6, row)
        inverse = 1.0 / (m + 0.3)
        const[0, row] = (0.5 * THIRD) * ice_row(5, row)
        const[1, row] = m * inverse
        const[2, row] = 0.075 * inverse
        const[3, row] = 0.3 * inverse * (ice_row(8, row) + ice_row(10, row))
        const[4, row] = 0.3 * inverse * (ice_row(9, row) + ice_row(11, row))

    lane = lax.broadcasted_iota(jnp.int32, (2, SUB, LANES), 2)
    is_last = lane == LANES - 1
    is_first = lane == 0

    def ahead_x(q):
        return jnp.where(is_last, 0.0, pltpu.roll(q, LANES - 1, 2) - q)

    def behind_x(q):
        return q - jnp.where(is_first, 0.0, pltpu.roll(q, 1, 2))

    def subcycle():
        for row in range(16):
            u, v = state[0, row], state[1, row]
            du_dx, dv_dx = ahead_x(u), ahead_x(v)
            if row < 15:
                du_dy, dv_dy = state[0, row + 1] - u, state[1, row + 1] - v
                div, ten, shr = du_dx + dv_dy, du_dx - dv_dy, du_dy + dv_dx
            else:
                div, ten, shr = du_dx, du_dx, dv_dx
            twice = div + div
            root = lax.rsqrt(twice * twice + ten * ten + shr * shr + 1.0)
            pressure = const[0, row]
            scaled = pressure * root
            state[2, row] = THIRD * state[2, row] + (scaled * twice - pressure)
            state[3, row] = THIRD * state[3, row] + scaled * ten
            state[4, row] = THIRD * state[4, row] + scaled * shr
        before_yy = None
        for row in range(16):
            one, two, xy = state[2, row], state[3, row], state[4, row]
            one = one + one
            xx, yy = one + two, one - two
            force_x, force_y = behind_x(xx), behind_x(xy)
            if row:
                force_x, force_y = force_x + (xy - state[4, row - 1]), force_y + (yy - before_yy)
            else:
                force_x, force_y = force_x + xy, force_y + yy
            before_yy = yy
            keep, push = const[1, row], const[2, row]
            u, v = state[0, row], state[1, row]
            state[0, row] = keep * (u + 0.09 * v) + (const[3, row] + push * force_x)
            state[1, row] = keep * (v - 0.09 * u) + (const[4, row] + push * force_y)

    def subcycles(first, last):
        @pl.loop(first, last, step=2)
        def _(step):
            subcycle()
            subcycle()

    subcycles(0, BEFORE_PACK)
    for field in range(fields):
        pl.loop(0, blocks)(lambda c, field=field: load(field, c).wait())
        packed = jnp.zeros((2 * SUB, LANES), jnp.float32)
        for level in range(levels):
            ends = jnp.where(
                lane16 < 2, qb[field, 0, level, 8:24, :], qb[field, blocks - 1, level, 8:24, :]
            )
            ends = pltpu.roll(ends, 4 * level + 2, 1)
            packed = jnp.where(lane16 // 4 == level, ends, packed)
        esend[field] = packed
        for group in range(groups):
            first = SLAB * SUB * group + 8

            @pl.loop(0, blocks, unroll=True)
            def _(c):
                for row in range(2):
                    sbuf[0, field, group, row, c] = flat[
                        field, c, pl.ds(first + 14 + row, SUB, stride=SLAB), :
                    ]
                    sbuf[1, field, group, row, c] = flat[
                        field, c, pl.ds(first + row, SUB, stride=SLAB), :
                    ]

        @pl.when(has_below)
        def _(field=field):
            if field == 0:
                meet()
            send(field)

    subcycles(BEFORE_PACK, BEFORE_FIRST_ROW)
    pl.when(jnp.logical_not(has_below))(exchange)
    subcycles(BEFORE_FIRST_ROW, SUBCYCLES)
    list_copy.wait()
    beta_copy.wait()
    prev_copy.wait()

    number = lax.broadcasted_iota(jnp.int32, (2, SUB, LANES), 0) * SUB + lax.broadcasted_iota(
        jnp.int32, (2, SUB, LANES), 1
    )
    covered = jnp.zeros((2, SUB, LANES), jnp.int32)
    for slot in range(blocks):
        block = jnp.where(slot < count[0], listed[slot], -1)
        covered = jnp.where(number == block, 1, covered)
    covered = covered > 0
    for row in range(16):
        u, v = state[0, row], state[1, row]
        one, two, xy = state[2, row], state[3, row], state[4, row]
        part = ice_row(7, row)
        results = {
            0: u,
            1: v,
            2: 0.5 * one + 0.25 * two,
            3: 0.5 * one - 0.25 * two,
            4: 0.25 * xy,
            8: part * (u - ice_row(10, row)) + (1.0 - part) * ice_row(8, row),
            9: part * (v - ice_row(11, row)) + (1.0 - part) * ice_row(9, row),
        }
        for n, result in results.items():
            result = jnp.where(covered, result, ice_row(n, row))
            for half in range(2):
                iceb[n, pl.ds(LANES * half + row, SUB, stride=16), :] = result[half]
    for c in range(blocks):
        span = slice(c * LANES, (c + 1) * LANES)
        for n in range(5):
            ice_out[n, :, span] = ice_view[n, c]
        for n in range(2):
            stress_out[n, :, span] = ice_view[8 + n, c]

    place = (tile * 16).astype(jnp.float32) + 0.5
    place = place + lax.broadcasted_iota(jnp.int32, (16, LANES), 0).astype(jnp.float32)
    coriolis = 0.2 * (2.0 * place / (16.0 * n_tile) - 1.0)

    def receive(field, group):
        @pl.when(group == 0)
        def _():
            for way in range(3):
                pl.when(edge_receives[way])(
                    lambda way=way: edge_copies(edge_refs, field, way, edge_peers).wait_recv()
                )

        first = pl.multiple_of(SLAB * SUB * group, SUB)

        def shifted(inner, x):
            return pltpu.roll(x, lax.rem(2 * LANES - 2 - 4 * (group * SUB + inner), LANES), 1)

        for direction, offset, corner in ((0, 6, 0), (1, 24, 24)):
            part = erecv.at[1, field, 8:16] if direction == 0 else erecv.at[2, field, 0:8]

            @pl.when(receives[direction])
            def _(direction=direction, offset=offset, corner=corner, part=part):
                copies(row_refs, direction, field, group, peers).wait_recv()

                @pl.loop(0, blocks, unroll=True)
                def _(c):
                    for row in range(2):
                        flat[field, c, pl.ds(first + offset + row, SUB, stride=SLAB), :] = rbuf[
                            direction, field, group, row, c
                        ]

                for inner in range(SUB):
                    qb[field, blocks, group * SUB + inner, corner : corner + 8, :] = shifted(
                        inner, part[...]
                    )

            @pl.when(jnp.logical_not(receives[direction]))
            def _(offset=offset):
                @pl.loop(0, blocks + 1)
                def _(c):
                    for row in range(2):
                        flat[field, c, pl.ds(first + offset + row, SUB, stride=SLAB), :] = (
                            jnp.zeros((SUB, LANES), jnp.float32)
                        )

        for inner in range(SUB):
            qb[field, blocks, group * SUB + inner, 8:24, :] = shifted(inner, erecv[0, field])

    @pl.loop(0, 2 * groups)
    def _(chunk):
        field = lax.div(chunk, groups)
        group = lax.rem(chunk, groups)
        receive(field, group)
        turn = jnp.where(field == 0, 1.0, -1.0) * coriolis
        for inner in range(SUB):
            level = group * SUB + inner

            def emit(c, span, mixed, level=level):
                ocean_out[field, level, :, span] = (
                    mixed + turn * qb[1 - field, c, level, 8:24, :]
                )

            ocean_level(qb.at[field], betav, level, emit)

        @pl.when(group == 0)
        def _():
            for c in range(blocks):
                span = slice(c * LANES, (c + 1) * LANES)
                ocean_out[field, 0, :, span] = ocean_out[field, 0, :, span] + prevv[field, :, span]

    pl.loop(0, groups)(lambda group: receive(2, group))

    @pl.loop(0, fields)
    def _(field):
        for way in range(3):
            pl.when(edge_sends[way])(
                lambda way=way: edge_copies(edge_refs, field, way, edge_peers).wait_send()
            )

        @pl.loop(0, groups)
        def _(group):
            for direction in range(2):
                pl.when(sends[direction])(
                    lambda direction=direction: copies(
                        row_refs, direction, field, group, peers
                    ).wait_send()
                )


def finish_kernel(
    ocean, ice, stress, qb, betav, ocean_out, ice_out, stress_out, stage, sem, stage_sem
):
    levels = ocean.shape[1]
    pieces = []
    for field in range(ocean.shape[0]):
        for half in range(2):
            span = pl.ds(half * (levels // 2), levels // 2)
            pieces.append((ocean.at[field, span], ocean_out.at[field, span]))
    pieces += [(ice, ice_out), (stress, stress_out)]
    started = [pltpu.make_async_copy(a, b, sem.at[n]) for n, (a, b) in enumerate(pieces)]
    for copy in started:
        copy.start()

    def stored(group):
        span = pl.ds(group * SUB, SUB)
        return pltpu.make_async_copy(stage.at[span], ocean_out.at[2, span], stage_sem.at[group])

    @pl.loop(0, levels // SUB)
    def _(group):
        for inner in range(SUB):
            level = group * SUB + inner

            def emit(c, span, mixed, level=level):
                stage[level, :, span] = mixed

            ocean_level(qb.at[2], betav, level, emit)
        stored(group).start()

    for copy in started:
        copy.wait()
    pl.loop(0, levels // SUB)(lambda group: stored(group).wait())


def per_device(
    ocean_state,
    biharmonic,
    prev_stress,
    ice_state,
    strength,
    ice_mass,
    ice_fraction,
    wind_stress,
    ice_count,
    ice_list,
):
    fields, levels, rows, cols = ocean_state.shape
    blocks, groups = cols // LANES, levels // SUB
    f32 = jnp.float32
    dma = pltpu.SemaphoreType.DMA
    body = functools.partial(kernel, lax.axis_size("tile"), lax.axis_size("grp"))
    out_spec = pl.BlockSpec(memory_space=pltpu.VMEM)
    held = pl.pallas_call(
        body,
        name="coupled",
        out_shape=[
            pltpu.VMEM((2, levels, rows, cols), f32),
            pltpu.VMEM(ice_state.shape, f32),
            pltpu.VMEM(wind_stress.shape, f32),
            pltpu.VMEM((fields, blocks + 1, levels, SLAB, LANES), f32),
            pltpu.VMEM((rows, cols), f32),
        ],
        in_specs=[pl.BlockSpec(memory_space=pltpu.HBM)] * 8
        + [pl.BlockSpec(memory_space=pltpu.SMEM), pl.BlockSpec(memory_space=pltpu.HBM)],
        out_specs=[out_spec] * 5,
        scratch_shapes=[
            pltpu.SMEM((blocks,), jnp.int32),
            pltpu.VMEM((2, rows, cols), f32),
            pltpu.VMEM((12, blocks * rows, LANES), f32),
            pltpu.VMEM((5, rows, 2, SUB, LANES), f32),
            pltpu.VMEM((5, rows, 2, SUB, LANES), f32),
            pltpu.VMEM((2, fields, groups, 2, blocks, SUB, LANES), f32),
            pltpu.VMEM((2, fields, groups, 2, blocks, SUB, LANES), f32),
            pltpu.VMEM((fields, rows, LANES), f32),
            pltpu.VMEM((3, fields, rows, LANES), f32),
            dma((fields, blocks)),
            dma((3,)),
            dma((6, blocks)),
            dma((2, fields, groups)),
            dma((2, fields, groups)),
            dma((3, fields)),
            dma((3, fields)),
        ],
        compiler_params=pltpu.CompilerParams(
            collective_id=0, has_side_effects=True, vmem_limit_bytes=KERNEL_LIMIT
        ),
    )(
        ocean_state,
        biharmonic,
        prev_stress,
        ice_state,
        strength,
        ice_mass,
        ice_fraction,
        wind_stress,
        ice_count,
        ice_list.reshape(-1),
    )
    return pl.pallas_call(
        finish_kernel,
        name="finish",
        out_shape=[
            jax.ShapeDtypeStruct(a.shape, a.dtype) for a in (ocean_state, ice_state, wind_stress)
        ],
        in_specs=[out_spec] * 5,
        out_specs=[pl.BlockSpec(memory_space=pltpu.HBM)] * 3,
        scratch_shapes=[pltpu.VMEM((levels, rows, cols), f32), dma((6,)), dma((groups,))],
        compiler_params=pltpu.CompilerParams(vmem_limit_bytes=FINISH_LIMIT),
    )(*[pltpu.with_memory_space_constraint(array, pltpu.VMEM) for array in held])


def solution(mesh):
    wide = P(None, "tile", "grp")
    flat = P("tile", "grp")
    deep = P(None, None, "tile", "grp")
    return jax.shard_map(
        per_device,
        mesh=mesh,
        in_specs=(
            deep,
            flat,
            wide,
            wide,
            flat,
            flat,
            flat,
            wide,
            P(("grp", "tile")),
            P(("grp", "tile"), None),
        ),
        out_specs=(deep, wide, wide),
        check_vma=False,
    )
```

```python
import functools

import jax
import jax.numpy as jnp
from jax import lax
from jax.experimental import pallas as pl
from jax.experimental.pallas import tpu as pltpu
from jax.sharding import PartitionSpec as P

MESH = pl.DeviceIdType.MESH
LANES = 128
SUB = 8
SLAB = 32
SUBCYCLES = 64
BEFORE_PACK = 2
KERNEL_LIMIT = 35 << 20
FINISH_LIMIT = 8 << 20
BEFORE_FIRST_ROW = 24
THIRD = 2.0 / 3.0


def copies(refs, direction, field, peers):
    sbuf, rbuf, ssem, rsem = refs
    return pltpu.make_async_remote_copy(
        src_ref=sbuf.at[direction, field],
        dst_ref=rbuf.at[direction, field],
        send_sem=ssem.at[direction, field],
        recv_sem=rsem.at[direction, field],
        device_id=peers[direction],
        device_id_type=MESH,
    )


def edge_copies(refs, field, way, peers):
    esend, erecv, essem, ersem = refs
    return pltpu.make_async_remote_copy(
        src_ref=esend.at[field],
        dst_ref=erecv.at[way, field],
        send_sem=essem.at[way, field],
        recv_sem=ersem.at[way, field],
        device_id=peers[way],
        device_id_type=MESH,
    )


def ocean_level(q, betav, level, emit):
    blocks, levels = q.shape[0] - 1, q.shape[1]
    lane = lax.broadcasted_iota(jnp.int32, (2 * SUB, LANES), 1)
    upper = jnp.maximum(level - 1, 0)
    lower = jnp.minimum(level + 1, levels - 1)

    def column(c):
        center = q[c, level, 8:24, :]
        near = q[c, level, 7:23, :] + q[c, level, 9:25, :]
        cross = near - 4.0 * center
        return (
            center,
            cross,
            pltpu.roll(center, 2, 1),
            pltpu.roll(center, LANES - 2, 1),
            pltpu.roll(cross, 1, 1),
            pltpu.roll(cross, LANES - 1, 1),
        )

    wrap = column(blocks)
    west, here = wrap, column(0)
    for c in range(blocks):
        east = column(c + 1) if c < blocks - 1 else wrap
        span = slice(c * LANES, (c + 1) * LANES)
        center, cross = here[0], here[1]
        far = q[c, level, 6:22, :] + q[c, level, 10:26, :]
        far = far + jnp.where(lane < 2, west[2], here[2])
        far = far + jnp.where(lane >= LANES - 2, east[3], here[3])
        near = jnp.where(lane < 1, west[4], here[4]) + jnp.where(
            lane >= LANES - 1, east[5], here[5]
        )
        near = near - 4.0 * cross
        smooth = (near + near) + (far - 12.0 * center)
        both = q[c, upper, 8:24, :] + q[c, lower, 8:24, :]
        emit(c, span, (0.6 * center + 0.2 * both) - betav[:, span] * smooth)
        west, here = here, east


def kernel(
    n_tile,
    n_grp,
    ocean,
    beta,
    prev,
    ice,
    strength,
    mass,
    fraction,
    wind,
    count,
    listed_hbm,
    ocean_out,
    ice_out,
    stress_out,
    qb,
    betav,
    listed,
    prevv,
    iceb,
    state,
    const,
    sbuf,
    rbuf,
    esend,
    erecv,
    qsem,
    bsem,
    isem,
    ssem,
    rsem,
    essem,
    ersem,
):
    fields, blocks, levels = ocean.shape[0], ocean.shape[3] // LANES, ocean.shape[1]
    groups = levels // SUB
    tile = lax.axis_index("tile")
    grp = lax.axis_index("grp")
    above = lax.rem(tile + 1, n_tile)
    below = lax.rem(tile + n_tile - 1, n_tile)
    other = lax.rem(grp + 1, n_grp)
    peers = [{"grp": grp, "tile": above}, {"grp": grp, "tile": below}]
    edge_peers = [
        {"grp": other, "tile": tile},
        {"grp": other, "tile": above},
        {"grp": other, "tile": below},
    ]
    row_refs = (sbuf, rbuf, ssem, rsem)
    edge_refs = (esend, erecv, essem, ersem)
    flat = qb.reshape(fields, blocks + 1, levels * SLAB, LANES)
    ice_view = iceb.reshape(12, blocks, 16, LANES)

    def columns(c):
        return pl.ds(pl.multiple_of(c * LANES, LANES), LANES)

    def load(field, c):
        return pltpu.make_async_copy(
            ocean.at[field, :, :, columns(c)], qb.at[field, c, :, 8:24, :], qsem.at[field, c]
        )

    def ice_loads(c):
        span = columns(c)
        pairs = [
            (ice.at[:, :, span], ice_view.at[0:5, c]),
            (strength.at[:, span], ice_view.at[5, c]),
            (mass.at[:, span], ice_view.at[6, c]),
            (fraction.at[:, span], ice_view.at[7, c]),
            (wind.at[:, :, span], ice_view.at[8:10, c]),
            (ocean.at[0:2, 0, :, span], ice_view.at[10:12, c]),
        ]
        return [pltpu.make_async_copy(s, d, isem.at[n, c]) for n, (s, d) in enumerate(pairs)]

    @pl.loop(0, blocks)
    def _(c):
        for copy in ice_loads(c):
            copy.start()

    for field in range(fields):
        pl.loop(0, blocks)(lambda c, field=field: load(field, c).start())

    beta_copy = pltpu.make_async_copy(beta, betav, bsem.at[0])
    prev_copy = pltpu.make_async_copy(prev, prevv, bsem.at[1])
    list_copy = pltpu.make_async_copy(listed_hbm, listed, bsem.at[2])
    list_copy.start()
    beta_copy.start()
    prev_copy.start()

    has_below = tile > 0
    has_above = tile < n_tile - 1
    always = tile >= 0
    sends = [has_above, has_below]
    receives = [has_below, has_above]
    edge_sends = [always, has_above, has_below]
    edge_receives = [always, has_below, has_above]

    barrier = pltpu.get_barrier_semaphore()
    for peer, exists in zip(peers + edge_peers, sends + edge_sends):

        @pl.when(exists)
        def _(peer=peer):
            pl.semaphore_signal(barrier, inc=1, device_id=peer, device_id_type=MESH)

    lane16 = lax.broadcasted_iota(jnp.int32, (2 * SUB, LANES), 1)
    def meet():
        pl.when(has_below & has_above)(lambda: pl.semaphore_wait(barrier, 5))
        pl.when(jnp.logical_not(has_below & has_above))(lambda: pl.semaphore_wait(barrier, 3))

    def send(field):
        for way in range(3):
            pl.when(edge_sends[way])(
                lambda way=way: edge_copies(edge_refs, field, way, edge_peers).start()
            )
        for direction in range(2):
            pl.when(sends[direction])(
                lambda direction=direction: copies(row_refs, direction, field, peers).start()
            )

    def exchange():
        meet()
        for field in range(fields):
            send(field)

    @pl.loop(0, blocks)
    def _(c):
        for copy in ice_loads(c):
            copy.wait()

    def ice_row(n, row):
        return jnp.stack(
            [iceb[n, pl.ds(LANES * half + row, SUB, stride=16), :] for half in range(2)]
        )

    for row in range(16):
        sxx, syy = ice_row(2, row), ice_row(3, row)
        state[0, row] = ice_row(0, row)
        state[1, row] = ice_row(1, row)
        state[2, row] = sxx + syy
        state[3, row] = 2.0 * (sxx - syy)
        state[4, row] = 4.0 * ice_row(4, row)
        m = ice_row(6, row)
        inverse = 1.0 / (m + 0.3)
        const[0, row] = (0.5 * THIRD) * ice_row(5, row)
        const[1, row] = m * inverse
        const[2, row] = 0.075 * inverse
        const[3, row] = 0.3 * inverse * (ice_row(8, row) + ice_row(10, row))
        const[4, row] = 0.3 * inverse * (ice_row(9, row) + ice_row(11, row))

    lane = lax.broadcasted_iota(jnp.int32, (2, SUB, LANES), 2)
    is_last = lane == LANES - 1
    is_first = lane == 0

    def ahead_x(q):
        return jnp.where(is_last, 0.0, pltpu.roll(q, LANES - 1, 2) - q)

    def behind_x(q):
        return q - jnp.where(is_first, 0.0, pltpu.roll(q, 1, 2))

    def subcycle():
        for row in range(16):
            u, v = state[0, row], state[1, row]
            du_dx, dv_dx = ahead_x(u), ahead_x(v)
            if row < 15:
                du_dy, dv_dy = state[0, row + 1] - u, state[1, row + 1] - v
                div, ten, shr = du_dx + dv_dy, du_dx - dv_dy, du_dy + dv_dx
            else:
                div, ten, shr = du_dx, du_dx, dv_dx
            twice = div + div
            root = lax.rsqrt(twice * twice + ten * ten + shr * shr + 1.0)
            pressure = const[0, row]
            scaled = pressure * root
            state[2, row] = THIRD * state[2, row] + (scaled * twice - pressure)
            state[3, row] = THIRD * state[3, row] + scaled * ten
            state[4, row] = THIRD * state[4, row] + scaled * shr
        before_yy = None
        for row in range(16):
            one, two, xy = state[2, row], state[3, row], state[4, row]
            one = one + one
            xx, yy = one + two, one - two
            force_x, force_y = behind_x(xx), behind_x(xy)
            if row:
                force_x, force_y = force_x + (xy - state[4, row - 1]), force_y + (yy - before_yy)
            else:
                force_x, force_y = force_x + xy, force_y + yy
            before_yy = yy
            keep, push = const[1, row], const[2, row]
            u, v = state[0, row], state[1, row]
            state[0, row] = keep * (u + 0.09 * v) + (const[3, row] + push * force_x)
            state[1, row] = keep * (v - 0.09 * u) + (const[4, row] + push * force_y)

    def subcycles(first, last):
        @pl.loop(first, last, step=2)
        def _(step):
            subcycle()
            subcycle()

    subcycles(0, BEFORE_PACK)
    for field in range(fields):
        pl.loop(0, blocks)(lambda c, field=field: load(field, c).wait())
        packed = jnp.zeros((2 * SUB, LANES), jnp.float32)
        for level in range(levels):
            ends = jnp.where(
                lane16 < 2, qb[field, 0, level, 8:24, :], qb[field, blocks - 1, level, 8:24, :]
            )
            ends = pltpu.roll(ends, 4 * level + 2, 1)
            packed = jnp.where(lane16 // 4 == level, ends, packed)
        esend[field] = packed
        for group in range(groups):
            first = SLAB * SUB * group + 8

            @pl.loop(0, blocks, unroll=True)
            def _(c):
                for row in range(2):
                    sbuf[0, field, group, row, c] = flat[
                        field, c, pl.ds(first + 14 + row, SUB, stride=SLAB), :
                    ]
                    sbuf[1, field, group, row, c] = flat[
                        field, c, pl.ds(first + row, SUB, stride=SLAB), :
                    ]

        @pl.when(has_below)
        def _(field=field):
            if field == 0:
                meet()
            send(field)

    subcycles(BEFORE_PACK, BEFORE_FIRST_ROW)
    pl.when(jnp.logical_not(has_below))(exchange)
    subcycles(BEFORE_FIRST_ROW, SUBCYCLES)
    list_copy.wait()
    beta_copy.wait()
    prev_copy.wait()

    number = lax.broadcasted_iota(jnp.int32, (2, SUB, LANES), 0) * SUB + lax.broadcasted_iota(
        jnp.int32, (2, SUB, LANES), 1
    )
    covered = jnp.zeros((2, SUB, LANES), jnp.int32)
    for slot in range(blocks):
        block = jnp.where(slot < count[0], listed[slot], -1)
        covered = jnp.where(number == block, 1, covered)
    covered = covered > 0
    for row in range(16):
        u, v = state[0, row], state[1, row]
        one, two, xy = state[2, row], state[3, row], state[4, row]
        part = ice_row(7, row)
        results = {
            0: u,
            1: v,
            2: 0.5 * one + 0.25 * two,
            3: 0.5 * one - 0.25 * two,
            4: 0.25 * xy,
            8: part * (u - ice_row(10, row)) + (1.0 - part) * ice_row(8, row),
            9: part * (v - ice_row(11, row)) + (1.0 - part) * ice_row(9, row),
        }
        for n, result in results.items():
            result = jnp.where(covered, result, ice_row(n, row))
            for half in range(2):
                iceb[n, pl.ds(LANES * half + row, SUB, stride=16), :] = result[half]
    for c in range(blocks):
        span = slice(c * LANES, (c + 1) * LANES)
        for n in range(5):
            ice_out[n, :, span] = ice_view[n, c]
        for n in range(2):
            stress_out[n, :, span] = ice_view[8 + n, c]

    place = (tile * 16).astype(jnp.float32) + 0.5
    place = place + lax.broadcasted_iota(jnp.int32, (16, LANES), 0).astype(jnp.float32)
    coriolis = 0.2 * (2.0 * place / (16.0 * n_tile) - 1.0)

    def receive(field, group):
        @pl.when(group == 0)
        def _():
            for way in range(3):
                pl.when(edge_receives[way])(
                    lambda way=way: edge_copies(edge_refs, field, way, edge_peers).wait_recv()
                )

        first = pl.multiple_of(SLAB * SUB * group, SUB)

        def shifted(inner, x):
            return pltpu.roll(x, lax.rem(2 * LANES - 2 - 4 * (group * SUB + inner), LANES), 1)

        for direction, offset, corner in ((0, 6, 0), (1, 24, 24)):
            part = erecv.at[1, field, 8:16] if direction == 0 else erecv.at[2, field, 0:8]

            @pl.when(receives[direction])
            def _(direction=direction, offset=offset, corner=corner, part=part):
                pl.when(group == 0)(
                    lambda: copies(row_refs, direction, field, peers).wait_recv()
                )

                @pl.loop(0, blocks, unroll=True)
                def _(c):
                    for row in range(2):
                        flat[field, c, pl.ds(first + offset + row, SUB, stride=SLAB), :] = rbuf[
                            direction, field, group, row, c
                        ]

                for inner in range(SUB):
                    qb[field, blocks, group * SUB + inner, corner : corner + 8, :] = shifted(
                        inner, part[...]
                    )

            @pl.when(jnp.logical_not(receives[direction]))
            def _(offset=offset):
                @pl.loop(0, blocks + 1)
                def _(c):
                    for row in range(2):
                        flat[field, c, pl.ds(first + offset + row, SUB, stride=SLAB), :] = (
                            jnp.zeros((SUB, LANES), jnp.float32)
                        )

        for inner in range(SUB):
            qb[field, blocks, group * SUB + inner, 8:24, :] = shifted(inner, erecv[0, field])

    @pl.loop(0, 2 * groups)
    def _(chunk):
        field = lax.div(chunk, groups)
        group = lax.rem(chunk, groups)
        receive(field, group)
        turn = jnp.where(field == 0, 1.0, -1.0) * coriolis
        for inner in range(SUB):
            level = group * SUB + inner

            def emit(c, span, mixed, level=level):
                ocean_out[field, level, :, span] = (
                    mixed + turn * qb[1 - field, c, level, 8:24, :]
                )

            ocean_level(qb.at[field], betav, level, emit)

        @pl.when(group == 0)
        def _():
            for c in range(blocks):
                span = slice(c * LANES, (c + 1) * LANES)
                ocean_out[field, 0, :, span] = ocean_out[field, 0, :, span] + prevv[field, :, span]

    pl.loop(0, groups)(lambda group: receive(2, group))

    @pl.loop(0, fields)
    def _(field):
        for way in range(3):
            pl.when(edge_sends[way])(
                lambda way=way: edge_copies(edge_refs, field, way, edge_peers).wait_send()
            )

        for direction in range(2):
            pl.when(sends[direction])(
                lambda direction=direction: copies(row_refs, direction, field, peers).wait_send()
            )


def finish_kernel(
    ocean, ice, stress, qb, betav, ocean_out, ice_out, stress_out, stage, sem, stage_sem
):
    levels = ocean.shape[1]
    pieces = []
    for field in range(ocean.shape[0]):
        for half in range(2):
            span = pl.ds(half * (levels // 2), levels // 2)
            pieces.append((ocean.at[field, span], ocean_out.at[field, span]))
    pieces += [(ice, ice_out), (stress, stress_out)]
    started = [pltpu.make_async_copy(a, b, sem.at[n]) for n, (a, b) in enumerate(pieces)]
    for copy in started:
        copy.start()

    def stored(group):
        span = pl.ds(group * SUB, SUB)
        return pltpu.make_async_copy(stage.at[span], ocean_out.at[2, span], stage_sem.at[group])

    @pl.loop(0, levels // SUB)
    def _(group):
        for inner in range(SUB):
            level = group * SUB + inner

            def emit(c, span, mixed, level=level):
                stage[level, :, span] = mixed

            ocean_level(qb.at[2], betav, level, emit)
        stored(group).start()

    for copy in started:
        copy.wait()
    pl.loop(0, levels // SUB)(lambda group: stored(group).wait())


def per_device(
    ocean_state,
    biharmonic,
    prev_stress,
    ice_state,
    strength,
    ice_mass,
    ice_fraction,
    wind_stress,
    ice_count,
    ice_list,
):
    fields, levels, rows, cols = ocean_state.shape
    blocks, groups = cols // LANES, levels // SUB
    f32 = jnp.float32
    dma = pltpu.SemaphoreType.DMA
    body = functools.partial(kernel, lax.axis_size("tile"), lax.axis_size("grp"))
    out_spec = pl.BlockSpec(memory_space=pltpu.VMEM)
    held = pl.pallas_call(
        body,
        name="coupled",
        out_shape=[
            pltpu.VMEM((2, levels, rows, cols), f32),
            pltpu.VMEM(ice_state.shape, f32),
            pltpu.VMEM(wind_stress.shape, f32),
            pltpu.VMEM((fields, blocks + 1, levels, SLAB, LANES), f32),
            pltpu.VMEM((rows, cols), f32),
        ],
        in_specs=[pl.BlockSpec(memory_space=pltpu.HBM)] * 8
        + [pl.BlockSpec(memory_space=pltpu.SMEM), pl.BlockSpec(memory_space=pltpu.HBM)],
        out_specs=[out_spec] * 5,
        scratch_shapes=[
            pltpu.SMEM((blocks,), jnp.int32),
            pltpu.VMEM((2, rows, cols), f32),
            pltpu.VMEM((12, blocks * rows, LANES), f32),
            pltpu.VMEM((5, rows, 2, SUB, LANES), f32),
            pltpu.VMEM((5, rows, 2, SUB, LANES), f32),
            pltpu.VMEM((2, fields, groups, 2, blocks, SUB, LANES), f32),
            pltpu.VMEM((2, fields, groups, 2, blocks, SUB, LANES), f32),
            pltpu.VMEM((fields, rows, LANES), f32),
            pltpu.VMEM((3, fields, rows, LANES), f32),
            dma((fields, blocks)),
            dma((3,)),
            dma((6, blocks)),
            dma((2, fields)),
            dma((2, fields)),
            dma((3, fields)),
            dma((3, fields)),
        ],
        compiler_params=pltpu.CompilerParams(
            collective_id=0, has_side_effects=True, vmem_limit_bytes=KERNEL_LIMIT
        ),
    )(
        ocean_state,
        biharmonic,
        prev_stress,
        ice_state,
        strength,
        ice_mass,
        ice_fraction,
        wind_stress,
        ice_count,
        ice_list.reshape(-1),
    )
    return pl.pallas_call(
        finish_kernel,
        name="finish",
        out_shape=[
            jax.ShapeDtypeStruct(a.shape, a.dtype) for a in (ocean_state, ice_state, wind_stress)
        ],
        in_specs=[out_spec] * 5,
        out_specs=[pl.BlockSpec(memory_space=pltpu.HBM)] * 3,
        scratch_shapes=[pltpu.VMEM((levels, rows, cols), f32), dma((6,)), dma((groups,))],
        compiler_params=pltpu.CompilerParams(vmem_limit_bytes=FINISH_LIMIT),
    )(*[pltpu.with_memory_space_constraint(array, pltpu.VMEM) for array in held])


def solution(mesh):
    wide = P(None, "tile", "grp")
    flat = P("tile", "grp")
    deep = P(None, None, "tile", "grp")
    return jax.shard_map(
        per_device,
        mesh=mesh,
        in_specs=(
            deep,
            flat,
            wide,
            wide,
            flat,
            flat,
            flat,
            wide,
            P(("grp", "tile")),
            P(("grp", "tile"), None),
        ),
        out_specs=(deep, wide, wide),
        check_vma=False,
    )
```
